128 devices in a mesh: depth: 8 (over z, core), cols: 16 (over x, y).
Axes of the slice: x: 4, y: 4, z: 4, core: 2. Of those that a mesh axis runs over, the one named last changes fastest.
Arguments:
- depth_cell: int32 [8, 16, 16384], P('depth', 'cols'), may hold values from 0 to 15
- column_cell: int32 [8, 16, 16384], P('depth', 'cols'), may hold values from 0 to 263
- row_cell: int32 [8, 16, 16384], P('depth', 'cols'), may hold values from 0 to 127
- mass: bfloat16 [8, 16, 16384], P('depth', 'cols'), may hold values from 2 to 32
- counts: int32 [8, 16], P('depth', 'cols'), may hold values from 1 to 16384, 131072 in all within a row
- diffusion: float32 [3], replicated, may hold values from 0.04 to 0.14
- tf_center: float32 [8], replicated, may hold values from 0.2 to 1.2
- tf_sharp: float32 [8], replicated, may hold values from 1 to 8
- tf_opacity: float32 [8], replicated, may hold values from 0.0015625 to 0.046875
- tf_shade: float32 [8], replicated, may hold values from 0.3 to 3
- tf_color: float32 [8, 3], replicated, may hold values from 0 to 1
Outputs:
- image: float32 [32, 4096, 128], P('depth', 'cols')
The draws below stay inside these ranges and needn't reach their ends.
Inputs may be any that keep to these rules, and one draw needn't show every extreme that they name: `counts`: some brick of every depth row holds exactly 16384 live particles.
All inputs are finite; a program needn't handle non-finite values. No bound on the sum of `counts` on one device may be relied on, other than what follows from the above.
Results may differ from the reference program's by a relative error of at most 0.0003.
Values sent between devices are 32-bit elements; how exact they have to be, the bound alone decides.
A program may use at most 64 MiB of HBM per device.

```python
import math
import jax
import jax.numpy as jnp
import numpy as np
from jax import lax

CZ = 16
CX = 256
CY = 128
RIM = 4
SLOTS = 16384
SMOOTH = 4
TFS = 8
NZ = 128
NX = 4096
NY = 128
N_DEPTH = 8
N_COLS = 16


def place_ends(result, stream_key, smallest, largest):
    longest = result.shape.index(max(result.shape))
    spots = []
    for shift in (0, 1):
        where = [jax.random.randint(jax.random.fold_in(stream_key, axis), (), 0, length) for axis, length in enumerate(result.shape)]
        where[longest] = (where[longest] + shift) % result.shape[longest]
        spots.append(tuple(where))
    return result.at[spots[0]].set(smallest).at[spots[1]].set(largest)


def steps_of(stream_key, shape, pieces, smallest, top_value):
    gain = 1.0
    for position, shards_of in pieces:
        heights = jax.random.uniform(jax.random.fold_in(jax.random.fold_in(stream_key, 6), position), (shards_of,), jnp.float32, smallest / len(pieces), top_value / len(pieces))
        gain = gain * jnp.repeat(jnp.exp(heights), shape[position] // shards_of).reshape((-1,) + (1,) * (len(shape) - 1 - position))
    return gain


def profile(number_of, total, reach, skew):
    portions = [(1 << 20) // math.isqrt(rank ** skew) + 1 for rank in range(2, number_of + 1)]
    surplus, given = total - reach - (number_of - 1), [1] * (number_of - 1)
    while surplus > 0:
        free = [i for i in range(number_of - 1) if given[i] < reach]
        whole, left = sum([portions[i] for i in free]), surplus
        for i in free:
            addition = min(reach - given[i], max(1, left * portions[i] // whole), surplus)
            given[i] = given[i] + addition
            surplus = surplus - addition
    return np.array([reach] + given)


def uneven(own_key, number_of, total, reach, slope):
    if number_of == 2:
        one = jax.random.randint(own_key, (), max(1, total - reach), min(reach, total - 1) + 1)
        return jnp.stack([one, total - one])
    tallies = jnp.asarray(profile(number_of, total, reach, slope), jnp.int32)
    couples = (number_of - 1) // 2
    source_of, receiver = tallies[1:1 + 2 * couples:2], tallies[2:2 + 2 * couples:2]
    slack = jnp.minimum(source_of - 1, reach - receiver)
    passed = jax.random.randint(jax.random.fold_in(own_key, 1), (couples,), 0, 1 << 20) % (slack + 1)
    tallies = tallies.at[1:1 + 2 * couples:2].set(source_of - passed).at[2:2 + 2 * couples:2].set(receiver + passed)
    return tallies[jax.random.permutation(jax.random.fold_in(own_key, 2), number_of)]


def setup_inputs(seed: int = 0) -> dict:
    arg_keys = jax.random.split(jax.random.key(seed), 12)
    return {
        "depth_cell": place_ends(jax.random.randint(arg_keys[0], (N_DEPTH, N_COLS, SLOTS), 0, CZ), jax.random.fold_in(arg_keys[0], 1), 0, CZ - 1).astype(jnp.int32),
        "column_cell": place_ends(jax.random.randint(arg_keys[1], (N_DEPTH, N_COLS, SLOTS), 0, CX + 2 * RIM), jax.random.fold_in(arg_keys[1], 1), 0, (CX + 2 * RIM) - 1).astype(jnp.int32),
        "row_cell": place_ends(jax.random.randint(arg_keys[2], (N_DEPTH, N_COLS, SLOTS), 0, CY), jax.random.fold_in(arg_keys[2], 1), 0, CY - 1).astype(jnp.int32),
        "mass": jnp.clip(jnp.exp(math.log(32.0) - 2.7725887 * jax.random.uniform(arg_keys[3], (N_DEPTH, N_COLS, SLOTS), jnp.float32) ** steps_of(arg_keys[3], (N_DEPTH, N_COLS, SLOTS), ((0, 8), (1, 16)), -0.2, 0.2)), 2.0, 32.0).astype(jnp.bfloat16),
        "counts": jax.vmap(lambda own: uneven(own, N_COLS, N_COLS * SLOTS // 2, SLOTS, 2))(jax.random.split(arg_keys[4], N_DEPTH)).reshape((N_DEPTH, N_COLS)).astype(jnp.int32),
        "diffusion": jnp.clip(jax.random.uniform(arg_keys[5], (3,), jnp.float32, 0.04, 0.14), 0.04, 0.14),
        "tf_center": jnp.clip(jax.random.uniform(arg_keys[6], (TFS,), jnp.float32, 0.2, 1.2), 0.2, 1.2),
        "tf_sharp": jnp.clip(jnp.exp(jax.random.uniform(arg_keys[7], (TFS,), jnp.float32, math.log(1.0), math.log(8.0))), 1.0, 8.0),
        "tf_opacity": jnp.clip(jnp.exp(jax.random.uniform(arg_keys[8], (TFS,), jnp.float32, math.log(0.0015625), math.log(0.046875))), 0.0015625, 0.046875),
        "tf_shade": jnp.clip(jnp.exp(jax.random.uniform(arg_keys[9], (TFS,), jnp.float32, math.log(0.3), math.log(3.0))), 0.3, 3.0),
        "tf_color": jnp.clip(jax.random.uniform(arg_keys[10], (TFS, 3), jnp.float32, 0.0, 1.0), 0.0, 1.0),
    }


def smooth_once(density, padded, diffusion):
    along_depth = padded[2:, 1:-1, 1:-1] + padded[:-2, 1:-1, 1:-1] - 2.0 * density
    along_column = padded[1:-1, 2:, 1:-1] + padded[1:-1, :-2, 1:-1] - 2.0 * density
    along_row = padded[1:-1, 1:-1, 2:] + padded[1:-1, 1:-1, :-2] - 2.0 * density
    return density + diffusion[0] * along_depth + diffusion[1] * along_column + diffusion[2] * along_row


def gradient_square(padded):
    slope_depth = (padded[2:, 1:-1, 1:-1] - padded[:-2, 1:-1, 1:-1]) * 0.5
    slope_column = (padded[1:-1, 2:, 1:-1] - padded[1:-1, :-2, 1:-1]) * 0.5
    slope_row = (padded[1:-1, 1:-1, 2:] - padded[1:-1, 1:-1, :-2]) * 0.5
    return slope_depth * slope_depth + slope_column * slope_column + slope_row * slope_row


def render(density, grad_square, center, sharpness, opacity, shade, tint):
    opaque = opacity * jax.nn.sigmoid(sharpness * (density - center))
    log_keep = jnp.log1p(-opaque)
    running_log = jnp.cumsum(log_keep, axis=0)
    weight = jnp.exp(running_log - log_keep) * opaque
    sum_density = jnp.sum(weight * density, axis=0)
    sum_gradient = jnp.sum(weight * grad_square, axis=0)
    colors = tint[:, None, None] * sum_density[None] + shade * sum_gradient[None]
    return jnp.concatenate([colors, jnp.exp(running_log[-1])[None]], axis=0)


def reference(depth_cell, column_cell, row_cell, mass, counts, diffusion, tf_center, tf_sharp, tf_opacity, tf_shade, tf_color):
    depth_index = jnp.arange(N_DEPTH, dtype=jnp.int32)[:, None, None]
    column_index = jnp.arange(N_COLS, dtype=jnp.int32)[None, :, None]
    slot_index = jnp.arange(SLOTS, dtype=jnp.int32)[None, None, :]
    global_depth = depth_index * CZ + depth_cell
    global_column = column_index * CX + column_cell - RIM
    usable = (slot_index < counts[:, :, None]) & (global_column >= 0) & (global_column < NX)
    flat_index = (global_depth * NX + global_column) * NY + row_cell
    flat_index = jnp.where(usable, flat_index, NZ * NX * NY).astype(jnp.int32)
    summed = jax.ops.segment_sum(mass.astype(jnp.float32).reshape(-1), flat_index.reshape(-1), num_segments=NZ * NX * NY + 1)
    density = summed[:-1].reshape(NZ, NX, NY)
    for sweep_index in range(SMOOTH):
        density = smooth_once(density, jnp.pad(density, 1), diffusion)
    grad_square = gradient_square(jnp.pad(density, 1))

    def one_function(params):
        center, sharpness, opacity, shade, tint = params
        return render(density, grad_square, center, sharpness, opacity, shade, tint)

    pictures = lax.map(one_function, (tf_center, tf_sharp, tf_opacity, tf_shade, tf_color))
    return pictures.reshape(4 * TFS, NX, NY)
```

```python
import jax, jax.numpy as jnp
from jax import lax
from jax.experimental import pallas as pl
from jax.experimental.pallas import tpu as pltpu
from jax.sharding import PartitionSpec as P

CZ, CX, CY, RIM = 16, 256, 128, 4
SMOOTH, TFS = 4, 8
HALO = SMOOTH + 1
DEEP = CZ + 2 * HALO
PLANE = 288
XO = 16
ROWS = CZ * PLANE
WIN = 64
UNROLL = 8
NBLK = 128

def exchange(x, stride, axis, bit):
    size = x.shape[axis]
    up = pltpu.roll(x, size - stride, axis)
    down = up if 2 * stride == size else pltpu.roll(x, stride, axis)
    return jnp.where(bit, jnp.maximum(x, down), jnp.minimum(x, up))

def bitonic(vs):
    lane = lax.broadcasted_iota(jnp.int32, (8, 128), 1)
    sub = lax.broadcasted_iota(jnp.int32, (8, 128), 0)
    def bit_of(j, i):
        if j < 4:
            return (i >> j) & 1
        if j < 7:
            return (sub >> (j - 4)) & 1
        return (lane >> (j - 7)) & 1
    hot = {j: bit_of(j, 0) == 1 for j in range(4, 14)}
    neg = {j: -bit_of(j, 0) for j in range(4, 14)}
    def flips(j, i):
        if j == 0 or j == 14:
            return 0
        if j < 4:
            return -((i >> j) & 1)
        return neg[j]
    for k in range(1, 15):
        out = []
        for i, v in enumerate(vs):
            a, b = flips(k - 1, i), flips(k, i)
            if isinstance(a, int) and isinstance(b, int):
                v = ~v if a != b else v
            else:
                v = v ^ (a ^ b)
            out.append(v)
        vs = out
        for j in range(k - 1, -1, -1):
            if j < 4:
                out = list(vs)
                for i in range(16):
                    p = i ^ (1 << j)
                    if i < p:
                        out[i] = jnp.minimum(vs[i], vs[p])
                        out[p] = jnp.maximum(vs[i], vs[p])
                vs = out
            elif j < 7:
                vs = [exchange(v, 1 << (j - 4), 0, hot[j]) for v in vs]
            else:
                vs = [exchange(v, 1 << (j - 7), 1, hot[j]) for v in vs]
    return vs

def deposit_kernel(key_ref, out_ref, raw, tidy, ends, sem):
    vs = bitonic([key_ref[8 * i : 8 * i + 8, :] for i in range(16)])
    for i in range(16):
        raw[8 * i : 8 * i + 8, :] = vs[i]
    first = pltpu.make_async_copy(raw.at[pl.ds(0, 8)], ends.at[0], sem.at[0])
    last = pltpu.make_async_copy(raw.at[pl.ds(120, 8)], ends.at[1], sem.at[1])
    first.start()
    last.start()
    tidy[...] = raw[...].T
    zeros = jnp.zeros((PLANE, 128), jnp.float32)

    @pl.loop(0, CZ)
    def _(z):
        out_ref[pl.ds(pl.multiple_of(z * PLANE, 8), PLANE), :] = zeros

    first.wait()
    last.wait()
    ys = lax.broadcasted_iota(jnp.int32, (128, 128), 0)
    ws = lax.broadcasted_iota(jnp.int32, (WIN, 128), 0)

    def window(row, start, y_hot):
        hot = jnp.where(ws == row - start, 1.0, 0.0).astype(jnp.bfloat16)
        return lax.dot_general(hot, y_hot, (((1,), (1,)), ((), ())), preferred_element_type=jnp.float32)

    def y_part(b):
        keys = tidy[pl.ds(b, 1), :]
        mass = (keys & 4095).astype(jnp.float32) * (1.0 / 64.0)
        y = (keys >> 12) & 127
        y_hot = jnp.where(ys == y, mass, 0.0).astype(jnp.bfloat16)
        return (keys >> 19) + 4096, y_hot

    def bounds(b):
        lo = (ends[0, 0, b] >> 19) + 4096
        hi = (ends[1, 7, b] >> 19) + 4096
        start = jnp.minimum((lo >> 3) << 3, ROWS - WIN)
        return pl.multiple_of(start, 8), (hi - start) >> 6

    @pl.loop(0, NBLK // UNROLL)
    def _(g):
        extra = 0
        parts = []
        for u in range(UNROLL):
            b = g * UNROLL + u
            start, more = bounds(b)
            row, y_hot = y_part(b)
            parts.append((start, window(row, start, y_hot)))
            extra = extra + more
        for start, part in parts:
            out_ref[pl.ds(start, WIN), :] += part

        @pl.when(extra > 0)
        def _():
            for u in range(UNROLL):
                b = g * UNROLL + u
                start, more = bounds(b)

                @pl.loop(0, more)
                def _(n):
                    place = pl.multiple_of(jnp.minimum(start + (n + 1) * WIN, ROWS - WIN), 8)
                    skip = start + (n + 1) * WIN - place
                    row, y_hot = y_part(b)
                    row = jnp.where(row - place >= skip, row, -1)
                    out_ref[pl.ds(place, WIN), :] += window(row, place, y_hot)

def keys_of(depth_cell, column_cell, row_cell, mass, count):
    slot = jnp.arange(16384, dtype=jnp.int32)
    weight = jnp.where(slot < count, mass.astype(jnp.float32) * 64.0, 0.0).astype(jnp.int32)
    row = depth_cell * PLANE + column_cell + (XO - RIM) - 4096
    return ((row << 19) | (row_cell << 12) | weight).reshape(128, 128)

def deposit(key):
    return pl.pallas_call(
        deposit_kernel,
        out_shape=jax.ShapeDtypeStruct((ROWS, 128), jnp.float32),
        in_specs=[pl.BlockSpec(memory_space=pltpu.VMEM)],
        out_specs=pl.BlockSpec(memory_space=pltpu.VMEM),
        scratch_shapes=[
            pltpu.VMEM((128, 128), jnp.int32),
            pltpu.VMEM((128, 128), jnp.int32),
            pltpu.SMEM((2, 8, 128), jnp.int32),
            pltpu.SemaphoreType.DMA((2,)),
        ],
        name="deposit",
    )(key)


def lanes_of():
    lane = lax.broadcasted_iota(jnp.int32, (8, 128), 1)
    return jnp.where(lane == 0, 0.0, 1.0), jnp.where(lane == 127, 0.0, 1.0)

def sweep(src, dst, lo, hi, coef, z_live, x_live):
    has_left, has_right = lanes_of()
    center, d0, d1, d2 = coef

    @pl.loop(lo, hi)
    def _(z):
        live = z_live(z)
        c, a, b = center * live, d0 * live, d1 * live
        left, right = has_left * (d2 * live), has_right * (d2 * live)
        for n in range(34):
            r = 8 + 8 * n
            v = src[z, r : r + 8, :]
            along_z = src[z - 1, r : r + 8, :] + src[z + 1, r : r + 8, :]
            along_x = src[z, r - 1 : r + 7, :] + src[z, r + 1 : r + 9, :]
            new = v * c + along_z * a + along_x * b
            new = new + pltpu.roll(v, 1, 1) * left + pltpu.roll(v, 127, 1) * right
            if n == 0:
                new = new * x_live[0]
            if n == 33:
                new = new * x_live[1]
            dst[z, r : r + 8, :] = new

def gradient(src, dst):
    has_left, has_right = lanes_of()
    left, right = has_left * 0.5, has_right * 0.5

    @pl.loop(0, CZ)
    def _(z):
        for n in range(32):
            r = XO + 8 * n
            v = src[z + HALO, r : r + 8, :]
            gz = (src[z + HALO + 1, r : r + 8, :] - src[z + HALO - 1, r : r + 8, :]) * 0.5
            gx = (src[z + HALO, r + 1 : r + 9, :] - src[z + HALO, r - 1 : r + 7, :]) * 0.5
            gy = pltpu.roll(v, 127, 1) * right - pltpu.roll(v, 1, 1) * left
            dst[z, 8 * n : 8 * n + 8, :] = gz * gz + gx * gx + gy * gy

def render(dens, grad, out, tf_ref, functions):
    @pl.loop(0, CX // 8)
    def _(n):
        r = pl.multiple_of(8 * n, 8)
        keep = {k: jnp.ones((8, 128), jnp.float32) for k in functions}
        sums = {k: None for k in functions}
        for z in range(CZ):
            d = dens[z + HALO, pl.ds(r + XO, 8), :]
            g = grad[z, pl.ds(r, 8), :]
            for k in functions:
                t = jnp.tanh(d * tf_ref[0, k] + tf_ref[1, k])
                opaque = t * tf_ref[2, k] + tf_ref[2, k]
                w = keep[k] * opaque
                keep[k] = keep[k] - w
                if sums[k] is None:
                    sums[k] = (w * d, w * g)
                else:
                    sums[k] = (sums[k][0] + w * d, sums[k][1] + w * g)
        for k in functions:
            out[k, 0, pl.ds(r, 8), :] = sums[k][0]
            out[k, 1, pl.ds(r, 8), :] = sums[k][1]
            out[k, 2, pl.ds(r, 8), :] = keep[k]

def local_kernel(par_ref, tf_ref, low, mid, high, out, one, two, grad, sem):
    copies = [
        pltpu.make_async_copy(mid, one.at[pl.ds(HALO, CZ)], sem.at[0]),
        pltpu.make_async_copy(low, one.at[pl.ds(0, HALO)], sem.at[1]),
        pltpu.make_async_copy(high, one.at[pl.ds(HALO + CZ, HALO)], sem.at[2]),
    ]
    for copy in copies:
        copy.start()
    x_live = (par_ref[4], par_ref[5])
    coef = tuple(par_ref[i] for i in range(4))
    zeros = jnp.zeros((8, 128), jnp.float32)

    @pl.loop(0, DEEP)
    def _(z):
        two[z, 0:8, :] = zeros
        two[z, 280:288, :] = zeros
    for copy in copies:
        copy.wait()

    @pl.loop(0, DEEP)
    def _(z):
        one[z, 8:16, :] = one[z, 8:16, :] * x_live[0]
        one[z, 272:280, :] = one[z, 272:280, :] * x_live[1]

    def z_live(z):
        return jnp.where(z < HALO, par_ref[6], jnp.where(z >= HALO + CZ, par_ref[7], 1.0))

    src, dst = one, two
    for s in range(SMOOTH):
        sweep(src, dst, s + 1, DEEP - s - 1, coef, z_live, x_live)
        src, dst = dst, src
    gradient(src, grad)
    render(src, grad, out, tf_ref, range(TFS))

def local(par, tf, low, mid, high):
    smem = pl.BlockSpec(memory_space=pltpu.SMEM)
    any_ = pl.BlockSpec(memory_space=pl.ANY)
    return pl.pallas_call(
        local_kernel,
        out_shape=jax.ShapeDtypeStruct((TFS, 3, CX, CY), jnp.float32),
        in_specs=[smem, smem, any_, any_, any_],
        out_specs=pl.BlockSpec(memory_space=pltpu.VMEM),
        scratch_shapes=[
            pltpu.VMEM((DEEP, PLANE, CY), jnp.float32),
            pltpu.VMEM((DEEP, PLANE, CY), jnp.float32),
            pltpu.VMEM((CZ, CX, CY), jnp.float32),
            pltpu.SemaphoreType.DMA((3,)),
        ],
        compiler_params=pltpu.CompilerParams(vmem_limit_bytes=48 << 20),
        name="local",
    )(par, tf, low, mid, high)


def passed_along(array, axis, by):
    length = lax.axis_size(axis)
    pairs = [(i, i + by) for i in range(length) if 0 <= i + by < length]
    return lax.ppermute(array, axis, pairs)


def from_partner(value, axis, distance):
    pairs = [(source, source ^ distance) for source in range(lax.axis_size(axis))]
    return lax.ppermute(value, axis, pairs)


def shards(depth_cell, column_cell, row_cell, mass, counts, diffusion, tf_center, tf_sharp, tf_opacity, tf_shade, tf_color):
    key = keys_of(
        depth_cell.reshape(-1), column_cell.reshape(-1), row_cell.reshape(-1), mass.reshape(-1), counts[0, 0]
    )
    extended = deposit(key).reshape(CZ, PLANE, CY)
    from_prev = passed_along(extended[:, 264:280], "cols", 1)
    from_next = passed_along(extended[:, 8:24], "cols", -1)
    extended = extended.at[:, 8:24].add(from_prev).at[:, 264:280].add(from_next)
    low = passed_along(extended[CZ - HALO :], "depth", 1)
    high = passed_along(extended[:HALO], "depth", -1)
    depth, cols = lax.axis_index("depth"), lax.axis_index("cols")
    lives = jnp.stack(
        [cols > 0, cols < lax.axis_size("cols") - 1, depth > 0, depth < lax.axis_size("depth") - 1]
    ).astype(jnp.float32)
    par = jnp.concatenate([1.0 - 2.0 * jnp.sum(diffusion, keepdims=True), diffusion, lives])
    tf = jnp.stack([0.5 * tf_sharp, -0.5 * tf_sharp * tf_center, 0.5 * tf_opacity])
    holding = local(par, tf, low, extended, high)
    for bit in (1, 2, 4):
        upper = (depth & bit) != 0
        half = holding.shape[0] // 2
        pairs = holding.reshape(half, 2, 3, CX, CY)
        kept = jnp.where(upper, pairs[:, 1], pairs[:, 0])
        sent = jnp.where(upper, pairs[:, 0], pairs[:, 1])
        came = from_partner(sent, "depth", bit)
        front, back = jnp.where(upper, came, kept), jnp.where(upper, kept, came)
        through = front[:, 2:]
        holding = jnp.concatenate([front[:, :2] + through * back[:, :2], through * back[:, 2:]], axis=1)
    dens, grad, keep = holding[0]
    tint = lax.dynamic_slice_in_dim(tf_color, depth, 1)[0]
    shade = lax.dynamic_slice_in_dim(tf_shade, depth, 1)
    colors = tint[:, None, None] * dens + shade[:, None, None] * grad
    return jnp.concatenate([colors, keep[None]], axis=0)


def solution(mesh):
    brick = P("depth", "cols", None)
    placed = (brick,) * 4 + (P("depth", "cols"),) + (P(),) * 6
    return jax.shard_map(shards, mesh=mesh, in_specs=placed, out_specs=brick, check_vma=False)
```

```python
import functools

import jax
import jax.numpy as jnp
import numpy as np
from jax import lax
from jax.experimental import pallas as pl
from jax.experimental.pallas import tpu as pltpu
from jax.sharding import PartitionSpec as P

CZ, CX, CY, RIM = 16, 256, 128, 4
SMOOTH, TFS = 4, 8
HALO = SMOOTH + 1
DEEP = CZ + 2 * HALO
PLANE = 288
XO = 16
ROWS = CZ * PLANE
WIN = 64
UNROLL = 8
SLOTS = 16384
NBLK = SLOTS // 128
MESH = pl.DeviceIdType.MESH
F32, BF16 = jnp.float32, jnp.bfloat16


def split(matrix):
    top = matrix.astype(BF16)
    return top, (matrix - top.astype(np.float64)).astype(BF16)


def tables():
    n = np.arange(1, CY + 1, dtype=np.float64)
    sine = np.sqrt(2.0 / (CY + 1)) * np.sin(np.pi * np.outer(n, n) / (CY + 1))
    slope = 0.5 * (np.eye(CY, k=-1) - np.eye(CY, k=1))
    s_top, s_low = split(sine)
    b_top, b_low = split(np.concatenate([sine, sine @ slope], axis=1))
    cosine = np.broadcast_to(2.0 * np.cos(np.pi * n / (CY + 1)), (8, CY)).astype(np.float32)
    return np.concatenate([s_top, s_top]), s_low, np.concatenate([b_top, b_top]), b_low, cosine


def apply(value, both, low):
    top = value.astype(BF16)
    rest = (value - top.astype(F32)).astype(BF16)
    return jnp.dot(jnp.concatenate([top, rest], axis=1), both, preferred_element_type=F32) + jnp.dot(
        top, low, preferred_element_type=F32
    )


def exchange(x, stride, axis, bit):
    size = x.shape[axis]
    up = pltpu.roll(x, size - stride, axis)
    down = up if 2 * stride == size else pltpu.roll(x, stride, axis)
    return jnp.where(bit, jnp.maximum(x, down), jnp.minimum(x, up))


def bitonic(vs):
    lane = lax.broadcasted_iota(jnp.int32, (8, 128), 1)
    sub = lax.broadcasted_iota(jnp.int32, (8, 128), 0)
    bits = {j: (sub >> (j - 4)) & 1 if j < 7 else (lane >> (j - 7)) & 1 for j in range(4, 14)}
    hot = {j: bits[j] == 1 for j in bits}
    neg = {j: -bits[j] for j in bits}

    def flips(j, i):
        if j == 0 or j == 14:
            return 0
        return -((i >> j) & 1) if j < 4 else neg[j]

    for k in range(1, 15):
        out = []
        for i, v in enumerate(vs):
            a, b = flips(k - 1, i), flips(k, i)
            if isinstance(a, int) and isinstance(b, int):
                out.append(~v if a != b else v)
            else:
                out.append(v ^ (a ^ b))
        vs = out
        for j in range(k - 1, -1, -1):
            if j >= 7:
                vs = [exchange(v, 1 << (j - 7), 1, hot[j]) for v in vs]
            elif j >= 4:
                vs = [exchange(v, 1 << (j - 4), 0, hot[j]) for v in vs]
            else:
                out = list(vs)
                for i in range(16):
                    p = i ^ (1 << j)
                    if i < p:
                        out[i] = jnp.minimum(vs[i], vs[p])
                        out[p] = jnp.maximum(vs[i], vs[p])
                vs = out
    return vs


def deposit_kernel(count, zc, xc, yc, mass, both, low, out, acc, wide, raw, tidy, ends, sem):
    for i in range(128):
        wide[i : i + 1, :] = mass[0, 0:1, 128 * i : 128 * i + 128].astype(F32)
    slot = 128 * lax.broadcasted_iota(jnp.int32, (8, 128), 0) + lax.broadcasted_iota(jnp.int32, (8, 128), 1)
    live = count[0, 0]
    keys = []
    for i in range(16):
        at = pl.ds(8 * i, 8)
        weight = jnp.where(slot + 1024 * i < live, wide[at, :] * 64.0, 0.0).astype(jnp.int32)
        row = zc[at, :] * PLANE + xc[at, :] + (XO - RIM - 4096)
        keys.append((row << 19) | (yc[at, :] << 12) | weight)
    keys = bitonic(keys)
    for i in range(16):
        raw[8 * i : 8 * i + 8, :] = keys[i]
    first = pltpu.make_async_copy(raw.at[pl.ds(0, 8)], ends.at[0], sem.at[0])
    last = pltpu.make_async_copy(raw.at[pl.ds(120, 8)], ends.at[1], sem.at[1])
    first.start()
    last.start()
    tidy[...] = raw[...].T
    zeros = jnp.zeros((PLANE, 128), F32)

    @pl.loop(0, CZ)
    def _(z):
        acc[pl.ds(pl.multiple_of(z * PLANE, 8), PLANE), :] = zeros

    first.wait()
    last.wait()
    ys = lax.broadcasted_iota(jnp.int32, (128, 128), 0)
    ws = lax.broadcasted_iota(jnp.int32, (WIN, 128), 0)

    def window(row, start, y_hot):
        hot = jnp.where(ws == row - start, 1.0, 0.0).astype(BF16)
        return lax.dot_general(hot, y_hot, (((1,), (1,)), ((), ())), preferred_element_type=F32)

    def block(b):
        key = tidy[pl.ds(b, 1), :]
        weight = (key & 4095).astype(F32) * (1.0 / 64.0)
        y_hot = jnp.where(ys == ((key >> 12) & 127), weight, 0.0).astype(BF16)
        return (key >> 19) + 4096, y_hot

    def bounds(b):
        lo = (ends[0, 0, b] >> 19) + 4096
        hi = (ends[1, 7, b] >> 19) + 4096
        start = jnp.minimum((lo >> 3) << 3, ROWS - WIN)
        return pl.multiple_of(start, 8), (hi - start) >> 6

    @pl.loop(0, NBLK // UNROLL)
    def _(g):
        extra = 0
        parts = []
        for u in range(UNROLL):
            b = g * UNROLL + u
            start, more = bounds(b)
            row, y_hot = block(b)
            parts.append((start, window(row, start, y_hot)))
            extra = extra + more
        for start, part in parts:
            acc[pl.ds(start, WIN), :] += part

        @pl.when(extra > 0)
        def _():
            for u in range(UNROLL):
                b = g * UNROLL + u
                start, more = bounds(b)

                @pl.loop(0, more)
                def _(n):
                    begin = start + (n + 1) * WIN
                    place = pl.multiple_of(jnp.minimum(begin, ROWS - WIN), 8)
                    row, y_hot = block(b)
                    row = jnp.where(row >= begin, row, -1)
                    acc[pl.ds(place, WIN), :] += window(row, place, y_hot)

    @pl.loop(0, CZ)
    def _(z):
        plane = acc[pl.ds(pl.multiple_of(z * PLANE, 8), PLANE), :]
        out[z] = apply(plane, both[...], low[...])


def deposit(count, zc, xc, yc, mass, both, low):
    smem = pl.BlockSpec(memory_space=pltpu.SMEM)
    vmem = pl.BlockSpec(memory_space=pltpu.VMEM)
    return pl.pallas_call(
        deposit_kernel,
        out_shape=jax.ShapeDtypeStruct((CZ, PLANE, CY), F32),
        in_specs=[smem] + [vmem] * 6,
        out_specs=vmem,
        scratch_shapes=[
            pltpu.VMEM((ROWS, CY), F32),
            pltpu.VMEM((128, 128), F32),
            pltpu.VMEM((128, 128), jnp.int32),
            pltpu.VMEM((128, 128), jnp.int32),
            pltpu.SMEM((2, 8, 128), jnp.int32),
            pltpu.SemaphoreType.DMA((2,)),
        ],
        name="deposit",
    )(count, zc, xc, yc, mass, both, low)


def sweep(src, dst, lo, hi, center, d0, d1, z_live, x_live):
    @pl.loop(lo, hi)
    def _(z):
        live = z_live(z)
        c, a, b = center * live, d0 * live, d1 * live
        for n in range(34):
            r = 8 + 8 * n
            along_z = src[z - 1, r : r + 8, :] + src[z + 1, r : r + 8, :]
            along_x = src[z, r - 1 : r + 7, :] + src[z, r + 1 : r + 9, :]
            new = src[z, r : r + 8, :] * c + along_z * a + along_x * b
            if n == 0:
                new = new * x_live[0]
            if n == 33:
                new = new * x_live[1]
            dst[z, r : r + 8, :] = new


def back_to_cells(src, dst, grad, both, low):
    @pl.loop(HALO - 1, HALO + CZ + 1)
    def _(z):
        mixed = apply(src[z, 8:280, :], both[...], low[...])
        dst[z, 8:280, :] = mixed[:, :CY]
        grad[z - HALO + 1] = mixed[8:264, CY:]


def gradient(src, grad):
    @pl.loop(0, CZ)
    def _(z):
        for n in range(32):
            r = XO + 8 * n
            gz = src[z + HALO + 1, r : r + 8, :] - src[z + HALO - 1, r : r + 8, :]
            gx = src[z + HALO, r + 1 : r + 9, :] - src[z + HALO, r - 1 : r + 7, :]
            gy = grad[z + 1, 8 * n : 8 * n + 8, :]
            grad[z + 1, 8 * n : 8 * n + 8, :] = (gz * gz + gx * gx) * 0.25 + gy * gy


def render(dens, grad, out, slope, shift, scale):
    @pl.loop(0, CX // 32)
    def _(n):
        r = pl.multiple_of(32 * n, 32)
        keep = jnp.ones((32, CY), F32)
        for z in range(CZ):
            d = dens[z + HALO, pl.ds(r + XO, 32), :]
            g = grad[z + 1, pl.ds(r, 32), :]
            t = jnp.tanh(d * slope + shift)
            w = keep * (t * scale + scale)
            keep = keep - w
            sum_d = w * d if z == 0 else sum_d + w * d
            sum_g = w * g if z == 0 else sum_g + w * g
        out[0, pl.ds(r, 32), :] = sum_d
        out[1, pl.ds(r, 32), :] = sum_g
        out[2, pl.ds(r, 32), :] = keep


def image_kernel(
    dif, tfc, tfs, tfo, cosine, both, low, ext, out,
    one, two, left, right, grad, mine, came, whole, local_sem, halo_send, halo_recv, pair_send, pair_recv, far_send, far_recv,
):
    depth, cols = lax.axis_index("depth"), lax.axis_index("cols")
    nd, nc = lax.axis_size("depth"), lax.axis_size("cols")
    core, chip = depth % 2, depth // 2
    chips = nd // 2
    partner = (depth + 1 - 2 * core, cols)

    def beside(dz, dx):
        return ((depth + dz + nd) % nd, (cols + dx + nc) % nc)

    around = [(dz, dx) for dz in (-1, 0, 1) for dx in (-1, 0, 1) if dz or dx]
    barrier = pltpu.get_barrier_semaphore()
    friends = [beside(dz, dx) for dz, dx in around] + [((depth + 2 * n) % nd, cols) for n in (1, 2, 3)]
    for friend in friends:
        pl.semaphore_signal(barrier, inc=1, device_id=friend, device_id_type=MESH)
    inner = pltpu.make_async_copy(ext, one.at[pl.ds(HALO, CZ)], local_sem)
    inner.start()
    zeros = jnp.zeros((8, CY), F32)

    @pl.loop(0, DEEP)
    def _(z):
        two[z, 0:8, :] = zeros
        two[z, 280:288, :] = zeros

    for z in (*range(HALO), *range(HALO + CZ, DEEP)):
        one[z, 0:8, :] = zeros
        one[z, 280:288, :] = zeros
    pl.semaphore_wait(barrier, len(friends))

    planes = {1: (CZ - HALO, 0, HALO), 0: (0, HALO, CZ), -1: (0, HALO + CZ, HALO)}
    copies = []
    for n, (dz, dx) in enumerate(around):
        src, dst, count = planes[dz]
        if dx == 0:
            source = ext.at[pl.ds(src, count), pl.ds(8, 272)]
            target = one.at[pl.ds(dst, count), pl.ds(8, 272)]
        elif dx == 1:
            source, target = ext.at[pl.ds(src, count), pl.ds(264, 16)], left.at[pl.ds(dst, count)]
        else:
            source, target = ext.at[pl.ds(src, count), pl.ds(8, 16)], right.at[pl.ds(dst, count)]
        copies.append(
            pltpu.make_async_remote_copy(
                src_ref=source, dst_ref=target, send_sem=halo_send.at[n], recv_sem=halo_recv.at[n],
                device_id=beside(dz, dx), device_id_type=MESH,
            )
        )
    for copy in copies:
        copy.start()
    inner.wait()
    for copy in copies:
        copy.wait()

    has_left = jnp.where(cols > 0, 1.0, 0.0)
    has_right = jnp.where(cols < nc - 1, 1.0, 0.0)
    has_low = jnp.where(depth > 0, 1.0, 0.0)
    has_high = jnp.where(depth < nd - 1, 1.0, 0.0)

    def z_live(z):
        return jnp.where(z < HALO, has_low, jnp.where(z >= HALO + CZ, has_high, 1.0))

    @pl.loop(0, DEEP)
    def _(z):
        one[z, 8:16, :] = (one[z, 8:16, :] + left[z, 0:8, :]) * has_left
        one[z, 16:24, :] = one[z, 16:24, :] + left[z, 8:16, :] * has_left
        one[z, 264:272, :] = one[z, 264:272, :] + right[z, 0:8, :] * has_right
        one[z, 272:280, :] = (one[z, 272:280, :] + right[z, 8:16, :]) * has_right

    @pl.when(depth == 0)
    def _():
        for z in range(HALO):
            one[z] = jnp.zeros((PLANE, CY), F32)

    @pl.when(depth == nd - 1)
    def _():
        for z in range(HALO + CZ, DEEP):
            one[z] = jnp.zeros((PLANE, CY), F32)

    d0, d1, d2 = dif[0], dif[1], dif[2]
    center = cosine[...] * d2 + (1.0 - 2.0 * (d0 + d1 + d2))
    src, dst = one, two
    for s in range(SMOOTH):
        sweep(src, dst, s + 1, DEEP - s - 1, center, d0, d1, z_live, (has_left, has_right))
        src, dst = dst, src
    back_to_cells(src, dst, grad, both, low)
    gradient(dst, grad)

    def draw(k, target):
        sharp = 0.5 * tfs[k]
        render(dst, grad, target, sharp, -sharp * tfc[k], 0.5 * tfo[k])

    swaps = []
    for j in range(chips):
        i = (chip + (2, 1, 3, 0)[j]) % chips
        draw(2 * i + 1 - core, mine.at[j])
        swap = pltpu.make_async_remote_copy(
            src_ref=mine.at[j], dst_ref=came.at[j], send_sem=pair_send.at[j], recv_sem=pair_recv.at[j],
            device_id=partner, device_id_type=MESH,
        )
        swap.start()
        swaps.append(swap)
    sends = []
    for j in range(chips):
        i = (chip + (2, 1, 3, 0)[j]) % chips
        held = mine.at[chips + j]
        draw(2 * i + core, held)
        swaps[j].wait_recv()
        place = held if j < chips - 1 else whole.at[chip]

        @pl.loop(0, CX // 32)
        def _(n):
            at = pl.ds(pl.multiple_of(32 * n, 32), 32)
            first = [jnp.where(core == 0, held[q, at, :], came[j, q, at, :]) for q in range(3)]
            then = [jnp.where(core == 0, came[j, q, at, :], held[q, at, :]) for q in range(3)]
            place[0, at, :] = first[0] + first[2] * then[0]
            place[1, at, :] = first[1] + first[2] * then[1]
            place[2, at, :] = first[2] * then[2]

        if j < chips - 1:
            send = pltpu.make_async_remote_copy(
                src_ref=held, dst_ref=whole.at[chip], send_sem=far_send.at[j], recv_sem=far_recv.at[j],
                device_id=(2 * i + core, cols), device_id_type=MESH,
            )
            send.start()
            sends.append(send)
    for send in sends:
        send.wait()
    for swap in swaps:
        swap.wait_send()

    @pl.loop(0, CX // 32)
    def _(n):
        at = pl.ds(pl.multiple_of(32 * n, 32), 32)
        sum_d, sum_g, keep = (whole[chips - 1, q, at, :] for q in range(3))
        for i in range(chips - 2, -1, -1):
            near = whole[i, 2, at, :]
            sum_d = whole[i, 0, at, :] + near * sum_d
            sum_g = whole[i, 1, at, :] + near * sum_g
            keep = near * keep
        out[0, at, :] = sum_d
        out[1, at, :] = sum_g
        out[2, at, :] = keep


def image(dif, tfc, tfs, tfo, cosine, both, low, ext):
    smem = pl.BlockSpec(memory_space=pltpu.SMEM)
    vmem = pl.BlockSpec(memory_space=pltpu.VMEM)
    return pl.pallas_call(
        image_kernel,
        out_shape=jax.ShapeDtypeStruct((3, CX, CY), F32),
        in_specs=[smem] * 4 + [vmem] * 3 + [pl.BlockSpec(memory_space=pl.ANY)],
        out_specs=vmem,
        scratch_shapes=[
            pltpu.VMEM((DEEP, PLANE, CY), F32),
            pltpu.VMEM((DEEP, PLANE, CY), F32),
            pltpu.VMEM((DEEP, 16, CY), F32),
            pltpu.VMEM((DEEP, 16, CY), F32),
            pltpu.VMEM((CZ + 2, CX, CY), F32),
            pltpu.VMEM((TFS, 3, CX, CY), F32),
            pltpu.VMEM((4, 3, CX, CY), F32),
            pltpu.VMEM((4, 3, CX, CY), F32),
            pltpu.SemaphoreType.DMA,
            pltpu.SemaphoreType.DMA((8,)),
            pltpu.SemaphoreType.DMA((8,)),
            pltpu.SemaphoreType.DMA((4,)),
            pltpu.SemaphoreType.DMA((4,)),
            pltpu.SemaphoreType.DMA((3,)),
            pltpu.SemaphoreType.DMA((3,)),
        ],
        compiler_params=pltpu.CompilerParams(collective_id=0, has_side_effects=True, vmem_limit_bytes=56 << 20),
        name="image",
    )(dif, tfc, tfs, tfo, cosine, both, low, ext)


def shards(depth_cell, column_cell, row_cell, mass, counts, diffusion, tf_center, tf_sharp, tf_opacity, tf_shade, tf_color):
    s_both, s_low, b_both, b_low, cosine = (jnp.asarray(table) for table in tables())
    cells = [cell.reshape(128, 128) for cell in (depth_cell, column_cell, row_cell)]
    extended = deposit(counts, *cells, mass, s_both, s_low)
    dens, grad, keep = image(diffusion, tf_center, tf_sharp, tf_opacity, cosine, b_both, b_low, extended)
    depth = lax.axis_index("depth")
    tint = lax.dynamic_slice_in_dim(tf_color, depth, 1)[0]
    shade = lax.dynamic_slice_in_dim(tf_shade, depth, 1)
    colors = tint[:, None, None] * dens + shade[:, None, None] * grad
    return jnp.concatenate([colors, keep[None]], axis=0)


def solution(mesh):
    brick = P("depth", "cols", None)
    placed = (brick,) * 4 + (P("depth", "cols"),) + (P(),) * 6
    return jax.shard_map(shards, mesh=mesh, in_specs=placed, out_specs=brick, check_vma=False)
```

```python
import functools

import jax
import jax.numpy as jnp
import numpy as np
from jax import lax
from jax.experimental import pallas as pl
from jax.experimental.pallas import tpu as pltpu
from jax.sharding import PartitionSpec as P

CZ, CX, CY, RIM = 16, 256, 128, 4
SMOOTH, TFS = 4, 8
HALO = SMOOTH + 1
DEEP = CZ + 2 * HALO
PLANE = 288
XO = 16
ROWS = CZ * PLANE
WIN = 64
UNROLL = 16
SLOTS = 16384
NBLK = SLOTS // 128
MESH = pl.DeviceIdType.MESH
F32, BF16 = jnp.float32, jnp.bfloat16


def split(matrix):
    top = matrix.astype(BF16)
    return top, (matrix - top.astype(np.float64)).astype(BF16)


def tables():
    n = np.arange(1, CY + 1, dtype=np.float64)
    sine = np.sqrt(2.0 / (CY + 1)) * np.sin(np.pi * np.outer(n, n) / (CY + 1))
    slope = 0.5 * (np.eye(CY, k=-1) - np.eye(CY, k=1))
    s_top, s_low = split(sine)
    b_top, b_low = split(np.concatenate([sine, sine @ slope], axis=1))
    cosine = np.broadcast_to(2.0 * np.cos(np.pi * n / (CY + 1)), (8, CY)).astype(np.float32)
    forth = np.block([[s_top, s_low], [s_top, np.zeros_like(s_low)]])
    return forth, np.concatenate([b_top, b_top]), b_low, cosine


def pair_of(value):
    top = value.astype(BF16)
    return top, (value - top.astype(F32)).astype(BF16)


def exchange(x, stride, axis, bit):
    size = x.shape[axis]
    up = pltpu.roll(x, size - stride, axis)
    down = up if 2 * stride == size else pltpu.roll(x, stride, axis)
    return jnp.where(bit, jnp.maximum(x, down), jnp.minimum(x, up))


def bitonic(vs):
    lane = lax.broadcasted_iota(jnp.int32, (8, 128), 1)
    sub = lax.broadcasted_iota(jnp.int32, (8, 128), 0)
    bits = {j: (sub >> (j - 4)) & 1 if j < 7 else (lane >> (j - 7)) & 1 for j in range(4, 14)}
    hot = {j: bits[j] == 1 for j in bits}
    neg = {j: -bits[j] for j in bits}

    def flips(j, i):
        if j == 0 or j == 14:
            return 0
        return -((i >> j) & 1) if j < 4 else neg[j]

    for k in range(1, 15):
        out = []
        for i, v in enumerate(vs):
            a, b = flips(k - 1, i), flips(k, i)
            if isinstance(a, int) and isinstance(b, int):
                out.append(~v if a != b else v)
            else:
                out.append(v ^ (a ^ b))
        vs = out
        for j in range(k - 1, 6 if k == 14 else -1, -1):
            if j >= 7:
                vs = [exchange(v, 1 << (j - 7), 1, hot[j]) for v in vs]
            elif j >= 4:
                vs = [exchange(v, 1 << (j - 4), 0, hot[j]) for v in vs]
            else:
                out = list(vs)
                for i in range(16):
                    p = i ^ (1 << j)
                    if i < p:
                        out[i] = jnp.minimum(vs[i], vs[p])
                        out[p] = jnp.maximum(vs[i], vs[p])
                vs = out
    return vs


def deposit_kernel(count, zc, xc, yc, mass, forth, out, acc, wide, raw, tidy, range_of, ends, sem):
    for i in range(128):
        wide[i : i + 1, :] = mass[0, 0:1, 128 * i : 128 * i + 128].astype(F32)
    slot = 128 * lax.broadcasted_iota(jnp.int32, (8, 128), 0) + lax.broadcasted_iota(jnp.int32, (8, 128), 1)
    live = count[0, 0]
    keys = []
    for i in range(16):
        at = pl.ds(8 * i, 8)
        weight = jnp.where(slot + 1024 * i < live, wide[at, :] * 64.0, 0.0).astype(jnp.int32)
        row = zc[at, :] * PLANE + xc[at, :] + (XO - RIM - 4096)
        keys.append((row << 19) | (yc[at, :] << 12) | weight)
    keys = bitonic(keys)
    for i in range(16):
        raw[8 * i : 8 * i + 8, :] = keys[i]
    range_of[0] = jnp.broadcast_to(jnp.min(functools.reduce(jnp.minimum, keys), axis=0, keepdims=True), (8, 128))
    range_of[1] = jnp.broadcast_to(jnp.max(functools.reduce(jnp.maximum, keys), axis=0, keepdims=True), (8, 128))
    tidy[...] = raw[...].T
    zeros = jnp.zeros((PLANE, 128), F32)

    @pl.loop(0, CZ)
    def _(z):
        acc[pl.ds(pl.multiple_of(z * PLANE, 8), PLANE), :] = zeros

    found = pltpu.make_async_copy(range_of, ends, sem)
    found.start()
    found.wait()
    ys = lax.broadcasted_iota(jnp.int32, (128, 128), 0)
    ws = lax.broadcasted_iota(jnp.int32, (WIN, 128), 0)

    def window(row, start, y_hot):
        hot = jnp.where(ws == row - start, 1.0, 0.0).astype(BF16)
        return lax.dot_general(hot, y_hot, (((1,), (1,)), ((), ())), preferred_element_type=F32)

    def block(b):
        key = tidy[pl.ds(b, 1), :]
        weight = (key & 4095).astype(F32) * (1.0 / 64.0)
        y_hot = jnp.where(ys == ((key >> 12) & 127), weight, 0.0).astype(BF16)
        return (key >> 19) + 4096, y_hot

    def bounds(b):
        lo = (ends[0, 0, b] >> 19) + 4096
        hi = (ends[1, 0, b] >> 19) + 4096
        start = jnp.minimum((lo >> 3) << 3, ROWS - WIN)
        return pl.multiple_of(start, 8), (hi - start) >> 6

    @pl.loop(0, NBLK // UNROLL)
    def _(g):
        extra = 0
        parts = []
        for u in range(UNROLL):
            b = g * UNROLL + u
            start, more = bounds(b)
            row, y_hot = block(b)
            parts.append((start, window(row, start, y_hot)))
            extra = extra + more
        for start, part in parts:
            acc[pl.ds(start, WIN), :] += part

        @pl.when(extra > 0)
        def _():
            @pl.loop(0, UNROLL)
            def _(u):
                b = g * UNROLL + u
                start, more = bounds(b)

                @pl.loop(0, more)
                def _(n):
                    begin = start + (n + 1) * WIN
                    place = pl.multiple_of(jnp.minimum(begin, ROWS - WIN), 8)
                    row, y_hot = block(b)
                    row = jnp.where(row >= begin, row, -1)
                    acc[pl.ds(place, WIN), :] += window(row, place, y_hot)

    @pl.loop(0, CZ)
    def _(z):
        plane = acc[pl.ds(pl.multiple_of(z * PLANE, 8), PLANE), :]
        both = jnp.dot(jnp.concatenate(pair_of(plane), axis=1), forth[...], preferred_element_type=F32)
        out[z] = both[:, :CY] + both[:, CY:]


def deposit(count, zc, xc, yc, mass, forth):
    smem = pl.BlockSpec(memory_space=pltpu.SMEM)
    vmem = pl.BlockSpec(memory_space=pltpu.VMEM)
    return pl.pallas_call(
        deposit_kernel,
        out_shape=jax.ShapeDtypeStruct((CZ, PLANE, CY), F32),
        in_specs=[smem] + [vmem] * 5,
        out_specs=vmem,
        scratch_shapes=[
            pltpu.VMEM((ROWS, CY), F32),
            pltpu.VMEM((128, 128), F32),
            pltpu.VMEM((128, 128), jnp.int32),
            pltpu.VMEM((128, 128), jnp.int32),
            pltpu.VMEM((2, 8, 128), jnp.int32),
            pltpu.SMEM((2, 8, 128), jnp.int32),
            pltpu.SemaphoreType.DMA,
        ],
        compiler_params=pltpu.CompilerParams(vmem_limit_bytes=12 << 20),
        name="deposit",
    )(count, zc, xc, yc, mass, forth)


CHUNK = 64
CHUNKS = CX // CHUNK
SPAN = CHUNK + 16
ORDER = (1, 2, 0, 3)
PARTS = ((64, 96), (160, 64), (8, 56), (224, 56))


def sweep(src, at, dst, lo, hi, center, d0, d1, z_live, x_live):
    @pl.loop(lo, hi, step=2)
    def _(base):
        for z in (base, base + 1):
            live = z_live(z)
            c, a, b = center * live, d0 * live, d1 * live
            for n in range(SPAN // 8):
                r = at + 8 * n
                along_z = src[z - 1, r : r + 8, :] + src[z + 1, r : r + 8, :]
                along_x = src[z, r - 1 : r + 7, :] + src[z, r + 1 : r + 9, :]
                new = src[z, r : r + 8, :] * c + along_z * a + along_x * b
                if n in x_live:
                    new = new * x_live[n]
                dst[z, 8 + 8 * n : 16 + 8 * n, :] = new


def back_to_cells(src, dst, grad, back, back_low):
    @pl.loop(0, (CZ + 2) // 2)
    def _(step):
        for half in range(2):
            z = step * 2 + half
            top, rest = pair_of(src[z + HALO - 1, 8 : 8 + SPAN, :])
            mixed = jnp.dot(jnp.concatenate([top, rest], axis=1), back[...], preferred_element_type=F32)
            mixed = mixed + jnp.dot(top, back_low[...], preferred_element_type=F32)
            dst[z + HALO - 1, 8 : 8 + SPAN, :] = mixed[:, :CY]
            grad[z] = mixed[8 : 8 + CHUNK, CY:]


def gradient(src, grad):
    @pl.loop(0, CZ // 2)
    def _(step):
        for half in range(2):
            z = step * 2 + half
            for n in range(CHUNK // 8):
                r = 16 + 8 * n
                gz = src[z + HALO + 1, r : r + 8, :] - src[z + HALO - 1, r : r + 8, :]
                gx = src[z + HALO, r + 1 : r + 9, :] - src[z + HALO, r - 1 : r + 7, :]
                gy = grad[z + 1, 8 * n : 8 * n + 8, :]
                grad[z + 1, 8 * n : 8 * n + 8, :] = (gz * gz + gx * gx) * 0.25 + gy * gy


def render(dens, grad, out, r, slope, shift, scale):
    keep = jnp.ones((32, CY), F32)
    for z in range(CZ):
        d = dens[z + HALO, pl.ds(r + 16, 32), :]
        g = grad[z + 1, pl.ds(r, 32), :]
        t = jnp.tanh(d * slope + shift)
        w = keep * (t * scale + scale)
        keep = keep - w
        sum_d = w * d if z == 0 else sum_d + w * d
        sum_g = w * g if z == 0 else sum_g + w * g
    out[0, pl.ds(r, 32), :] = sum_d
    out[1, pl.ds(r, 32), :] = sum_g
    out[2, pl.ds(r, 32), :] = keep


def image_kernel(
    dif, tfc, tfs, tfo, shade, tint, cosine, back, back_low, ext, out,
    one, ta, tb, left, right, grad, mine, came, whole,
    local_sem, side_send, side_recv, halo_send, halo_recv, pair_send, pair_recv, far_send, far_recv,
):
    depth, cols = lax.axis_index("depth"), lax.axis_index("cols")
    nd, nc = lax.axis_size("depth"), lax.axis_size("cols")
    core, chip = depth % 2, depth // 2
    chips = nd // 2
    partner = (depth + 1 - 2 * core, cols)

    def beside(dz, dx):
        return ((depth + dz + nd) % nd, (cols + dx + nc) % nc)

    around = [(dz, dx) for dz in (-1, 0, 1) for dx in (-1, 0, 1) if dz or dx]
    barrier = pltpu.get_barrier_semaphore()
    friends = [beside(dz, dx) for dz, dx in around] + [((depth + 2 * n) % nd, cols) for n in (1, 2, 3)]
    for friend in friends:
        pl.semaphore_signal(barrier, inc=1, device_id=friend, device_id_type=MESH)
    inner = pltpu.make_async_copy(ext, one.at[pl.ds(HALO, CZ)], local_sem)
    inner.start()
    zeros = jnp.zeros((8, CY), F32)

    @pl.loop(0, DEEP)
    def _(z):
        for t in (ta, tb):
            t[z, 0:8, :] = zeros
            t[z, 8 + SPAN : 16 + SPAN, :] = zeros

    for z in (*range(HALO), *range(HALO + CZ, DEEP)):
        one[z, 0:8, :] = zeros
        one[z, 280:288, :] = zeros
    pl.semaphore_wait(barrier, len(friends))

    planes = {1: (CZ - HALO, 0, HALO), 0: (0, HALO, CZ), -1: (0, HALO + CZ, HALO)}

    def copy_to(source, target, send, recv, device):
        copy = pltpu.make_async_remote_copy(
            src_ref=source, dst_ref=target, send_sem=send, recv_sem=recv, device_id=device, device_id_type=MESH
        )
        copy.start()
        return copy

    halos, sides = {}, {-1: [], 1: []}

    def send_halo(step):
        begin, rows = PARTS[step]
        for n, dz in enumerate((-1, 1)):
            src, dst, count = planes[dz]
            halos[step, dz] = copy_to(
                ext.at[pl.ds(src, count), pl.ds(begin, rows)], one.at[pl.ds(dst, count), pl.ds(begin, rows)],
                halo_send.at[step, n], halo_recv.at[step, n], beside(dz, 0),
            )

    send_halo(0)
    for n, (dz, dx) in enumerate((dz, dx) for dx in (1, -1) for dz in (-1, 0, 1)):
        src, dst, count = planes[dz]
        sides[dx].append(
            copy_to(
                ext.at[pl.ds(src, count), pl.ds(264 if dx == 1 else 8, 16)],
                (left if dx == 1 else right).at[pl.ds(dst, count)],
                side_send.at[n], side_recv.at[n], beside(dz, dx),
            )
        )
    for step in range(1, CHUNKS):
        send_halo(step)
    inner.wait()

    has_left = jnp.where(cols > 0, 1.0, 0.0)
    has_right = jnp.where(cols < nc - 1, 1.0, 0.0)
    has_low = jnp.where(depth > 0, 1.0, 0.0)
    has_high = jnp.where(depth < nd - 1, 1.0, 0.0)

    def z_live(z):
        return jnp.where(z < HALO, has_low, jnp.where(z >= HALO + CZ, has_high, 1.0))

    d0, d1, d2 = dif[0], dif[1], dif[2]
    center = cosine[...] * d2 + (1.0 - 2.0 * (d0 + d1 + d2))

    def assemble(step):
        begin, rows = PARTS[step]
        halos[step, -1].wait()
        halos[step, 1].wait()

        @pl.when(depth == 0)
        def _():
            for z in range(HALO):
                one[z, begin : begin + rows, :] = jnp.zeros((rows, CY), F32)

        @pl.when(depth == nd - 1)
        def _():
            for z in range(HALO + CZ, DEEP):
                one[z, begin : begin + rows, :] = jnp.zeros((rows, CY), F32)

        if ORDER[step] == 0:
            for copy in sides[1]:
                copy.wait()

            @pl.loop(0, DEEP)
            def _(z):
                live = z_live(z) * has_left
                one[z, 8:16, :] = one[z, 8:16, :] * has_left + left[z, 0:8, :] * live
                one[z, 16:24, :] = one[z, 16:24, :] + left[z, 8:16, :] * live

        if ORDER[step] == CHUNKS - 1:
            for copy in sides[-1]:
                copy.wait()

            @pl.loop(0, DEEP)
            def _(z):
                live = z_live(z) * has_right
                one[z, 264:272, :] = one[z, 264:272, :] + right[z, 0:8, :] * live
                one[z, 272:280, :] = one[z, 272:280, :] * has_right + right[z, 8:16, :] * live

    def draw(chunk, own):
        @pl.loop(0, chips * (CHUNK // 32))
        def _(n):
            j = n // (CHUNK // 32)
            r = pl.multiple_of((n % (CHUNK // 32)) * 32, 32)
            k = 2 * ((chip + j + 2) % chips) + (core if own else 1 - core)
            sharp = 0.5 * tfs[k]
            render(ta, grad, mine.at[chunk, j + (chips if own else 0)], r, sharp, -sharp * tfc[k], 0.5 * tfo[k])

    swaps, sends = {}, []

    def combine(chunk):
        swaps[chunk].wait_recv()
        for j in range(chips):
            i = (chip + j + 2) % chips
            held = mine.at[chunk, chips + j]
            place = whole.at[chip, chunk] if j == 2 else held
            for n in range(CHUNK // 32):
                at = pl.ds(32 * n, 32)
                first = [jnp.where(core == 0, held[q, at, :], came[chunk, j, q, at, :]) for q in range(3)]
                then = [jnp.where(core == 0, came[chunk, j, q, at, :], held[q, at, :]) for q in range(3)]
                place[0, at, :] = first[0] + first[2] * then[0]
                place[1, at, :] = first[1] + first[2] * then[1]
                place[2, at, :] = first[2] * then[2]
            if j != 2:
                m = j - j // 3
                sends.append(
                    copy_to(
                        held, whole.at[chip, chunk], far_send.at[chunk, m], far_recv.at[chunk, m],
                        (2 * i + core, cols),
                    )
                )

    for step in range(CHUNKS):
        chunk = ORDER[step]
        assemble(step)
        x_live = {0: has_left} if chunk == 0 else {SPAN // 8 - 1: has_right} if chunk == CHUNKS - 1 else {}
        sweep(one, 8 + CHUNK * chunk, ta, 1, DEEP - 1, center, d0, d1, z_live, x_live)
        sweep(ta, 8, tb, 2, DEEP - 2, center, d0, d1, z_live, x_live)
        if step:
            combine(ORDER[step - 1])
        sweep(tb, 8, ta, 3, DEEP - 3, center, d0, d1, z_live, x_live)
        sweep(ta, 8, tb, 4, DEEP - 4, center, d0, d1, z_live, x_live)
        back_to_cells(tb, ta, grad, back, back_low)
        gradient(ta, grad)
        draw(chunk, False)
        swaps[chunk] = copy_to(
            mine.at[chunk, pl.ds(0, chips)], came.at[chunk], pair_send.at[chunk], pair_recv.at[chunk], partner
        )
        draw(chunk, True)
    combine(ORDER[-1])

    color = [tint[q, depth] for q in range(3)]
    shading = shade[depth]
    for step in range(CHUNKS):
        for send in sends[3 * step : 3 * step + 3]:
            send.wait()
        chunk = ORDER[step]
        for n in range(CHUNK // 32):
            at = pl.ds(32 * n, 32)
            to = pl.ds(CHUNK * chunk + 32 * n, 32)
            sum_d, sum_g, keep = (whole[chips - 1, chunk, q, at, :] for q in range(3))
            for i in range(chips - 2, -1, -1):
                near = whole[i, chunk, 2, at, :]
                sum_d = whole[i, chunk, 0, at, :] + near * sum_d
                sum_g = whole[i, chunk, 1, at, :] + near * sum_g
                keep = near * keep
            for q in range(3):
                out[q, to, :] = sum_d * color[q] + sum_g * shading
            out[3, to, :] = keep
    for chunk in ORDER:
        swaps[chunk].wait_send()


def image(dif, tfc, tfs, tfo, shade, tint, cosine, back, back_low, ext):
    smem = pl.BlockSpec(memory_space=pltpu.SMEM)
    vmem = pl.BlockSpec(memory_space=pltpu.VMEM)
    return pl.pallas_call(
        image_kernel,
        out_shape=jax.ShapeDtypeStruct((4, CX, CY), F32),
        in_specs=[smem] * 6 + [vmem] * 3 + [pl.BlockSpec(memory_space=pl.ANY)],
        out_specs=vmem,
        scratch_shapes=[
            pltpu.VMEM((DEEP, PLANE, CY), F32),
            pltpu.VMEM((DEEP, SPAN + 16, CY), F32),
            pltpu.VMEM((DEEP, SPAN + 16, CY), F32),
            pltpu.VMEM((DEEP, 16, CY), F32),
            pltpu.VMEM((DEEP, 16, CY), F32),
            pltpu.VMEM((CZ + 2, CHUNK, CY), F32),
            pltpu.VMEM((CHUNKS, TFS, 3, CHUNK, CY), F32),
            pltpu.VMEM((CHUNKS, 4, 3, CHUNK, CY), F32),
            pltpu.VMEM((4, CHUNKS, 3, CHUNK, CY), F32),
            pltpu.SemaphoreType.DMA,
            pltpu.SemaphoreType.DMA((6,)),
            pltpu.SemaphoreType.DMA((6,)),
            pltpu.SemaphoreType.DMA((CHUNKS, 2)),
            pltpu.SemaphoreType.DMA((CHUNKS, 2)),
            pltpu.SemaphoreType.DMA((CHUNKS,)),
            pltpu.SemaphoreType.DMA((CHUNKS,)),
            pltpu.SemaphoreType.DMA((CHUNKS, 3)),
            pltpu.SemaphoreType.DMA((CHUNKS, 3)),
        ],
        compiler_params=pltpu.CompilerParams(collective_id=0, has_side_effects=True, vmem_limit_bytes=32 << 20),
        name="image",
    )(dif, tfc, tfs, tfo, shade, tint, cosine, back, back_low, ext)


def shards(depth_cell, column_cell, row_cell, mass, counts, diffusion, tf_center, tf_sharp, tf_opacity, tf_shade, tf_color):
    forth, back, back_low, cosine = (jnp.asarray(table) for table in tables())
    cells = [cell.reshape(128, 128) for cell in (depth_cell, column_cell, row_cell)]
    extended = deposit(counts, *cells, mass, forth)
    return image(
        diffusion, tf_center, tf_sharp, tf_opacity, tf_shade, tf_color.T, cosine, back, back_low, extended
    )


def solution(mesh):
    brick = P("depth", "cols", None)
    placed = (brick,) * 4 + (P("depth", "cols"),) + (P(),) * 6
    return jax.shard_map(shards, mesh=mesh, in_specs=placed, out_specs=brick, check_vma=False)
```

```python
import functools

import jax
import jax.numpy as jnp
import numpy as np
from jax import lax
from jax.experimental import pallas as pl
from jax.experimental.pallas import tpu as pltpu
from jax.sharding import PartitionSpec as P

CZ, CX, CY, RIM = 16, 256, 128, 4
SMOOTH, TFS = 4, 8
HALO = SMOOTH + 1
DEEP = CZ + 2 * HALO
PLANE = 288
XO = 16
ROWS = CZ * PLANE
WIN = 112
UNROLL = 8
SLOTS = 16384
NBLK = SLOTS // 256
MESH = pl.DeviceIdType.MESH
F32, BF16 = jnp.float32, jnp.bfloat16


def split(matrix):
    top = matrix.astype(BF16)
    return top, (matrix - top.astype(np.float64)).astype(BF16)


def tables():
    n = np.arange(1, CY + 1, dtype=np.float64)
    sine = np.sqrt(2.0 / (CY + 1)) * np.sin(np.pi * np.outer(n, n) / (CY + 1))
    slope = 0.5 * (np.eye(CY, k=-1) - np.eye(CY, k=1))
    s_top, s_low = split(sine)
    b_top, b_low = split(np.concatenate([sine, sine @ slope], axis=1))
    cosine = np.broadcast_to(2.0 * np.cos(np.pi * n / (CY + 1)), (8, CY)).astype(np.float32)
    forth = np.block([[s_top, s_low], [s_top, np.zeros_like(s_low)]])
    return forth, np.concatenate([b_top, b_top]), b_low, cosine


def pair_of(value):
    top = value.astype(BF16)
    return top, (value - top.astype(F32)).astype(BF16)


def exchange(x, stride, axis, bit):
    size = x.shape[axis]
    up = pltpu.roll(x, size - stride, axis)
    down = up if 2 * stride == size else pltpu.roll(x, stride, axis)
    return jnp.where(bit, jnp.maximum(x, down), jnp.minimum(x, up))


def bitonic(vs):
    lane = lax.broadcasted_iota(jnp.int32, (8, 128), 1)
    sub = lax.broadcasted_iota(jnp.int32, (8, 128), 0)
    bits = {j: (sub >> (j - 4)) & 1 if j < 7 else (lane >> (j - 7)) & 1 for j in range(4, 14)}
    hot = {j: bits[j] == 1 for j in bits}
    neg = {j: -bits[j] for j in bits}

    def flips(j, i):
        if j == 0 or j == 14:
            return 0
        return -((i >> j) & 1) if j < 4 else neg[j]

    for k in range(1, 15):
        out = []
        for i, v in enumerate(vs):
            a, b = flips(k - 1, i), flips(k, i)
            if isinstance(a, int) and isinstance(b, int):
                out.append(~v if a != b else v)
            else:
                out.append(v ^ (a ^ b))
        vs = out
        for j in range(k - 1, 6 if k == 14 else -1, -1):
            if j >= 7:
                vs = [exchange(v, 1 << (j - 7), 1, hot[j]) for v in vs]
            elif j >= 4:
                vs = [exchange(v, 1 << (j - 4), 0, hot[j]) for v in vs]
            else:
                out = list(vs)
                for i in range(16):
                    p = i ^ (1 << j)
                    if i < p:
                        out[i] = jnp.minimum(vs[i], vs[p])
                        out[p] = jnp.maximum(vs[i], vs[p])
                vs = out
    return vs


def deposit_kernel(count, zh, xh, yh, mh, fh, out, acc, zc, xc, yc, mass, forth, wide, raw, tidy, range_of, ends, sem):
    loads = [
        pltpu.make_async_copy(source, target, sem.at[n])
        for n, (source, target) in enumerate(((mh, mass), (zh, zc), (xh, xc), (yh, yc), (fh, forth)))
    ]
    for load in loads:
        load.start()
    zeros = jnp.zeros((PLANE, 128), F32)

    @pl.loop(0, CZ)
    def _(z):
        acc[pl.ds(pl.multiple_of(z * PLANE, 8), PLANE), :] = zeros

    loads[0].wait()
    for i in range(128):
        wide[i : i + 1, :] = mass[0, 0:1, 128 * i : 128 * i + 128].astype(F32)
    for load in loads[1:]:
        load.wait()
    slot = 128 * lax.broadcasted_iota(jnp.int32, (8, 128), 0) + lax.broadcasted_iota(jnp.int32, (8, 128), 1)
    live = count[0, 0]
    keys = []
    for i in range(16):
        at = pl.ds(8 * i, 8)
        weight = jnp.where(slot + 1024 * i < live, wide[at, :] * 64.0, 0.0).astype(jnp.int32)
        row = zc[at, :] * PLANE + xc[at, :] + (XO - RIM - 4096)
        keys.append((row << 19) | (yc[at, :] << 12) | weight)
    keys = bitonic(keys)
    range_of[0] = jnp.broadcast_to(jnp.min(functools.reduce(jnp.minimum, keys), axis=0, keepdims=True), (8, 128))
    range_of[1] = jnp.broadcast_to(jnp.max(functools.reduce(jnp.maximum, keys), axis=0, keepdims=True), (8, 128))
    found = pltpu.make_async_copy(range_of, ends, sem.at[5])
    found.start()
    for i in range(16):
        raw[8 * i : 8 * i + 8, :] = keys[i]
    tidy[...] = raw[...].T
    found.wait()
    ys = lax.broadcasted_iota(jnp.int32, (128, 128), 0)
    ws = lax.broadcasted_iota(jnp.int32, (WIN, 128), 0)

    def block(b, start, begin):
        hots, y_hots = [], []
        for half in range(2):
            key = tidy[pl.ds(2 * b + half, 1), :]
            row = (key >> 19) + 4096
            if begin is not None:
                row = jnp.where(row >= begin, row, -1)
            hots.append(jnp.where(ws == row - start, 1.0, 0.0).astype(BF16))
            weight = (key & 4095).astype(F32) * (1.0 / 64.0)
            y_hots.append(jnp.where(ys == ((key >> 12) & 127), weight, 0.0).astype(BF16))
        hot, y_hot = jnp.concatenate(hots, axis=1), jnp.concatenate(y_hots, axis=1)
        return lax.dot_general(hot, y_hot, (((1,), (1,)), ((), ())), preferred_element_type=F32)

    def bounds(b):
        lo = (ends[0, 0, 2 * b] >> 19) + 4096
        hi = (ends[1, 0, 2 * b + 1] >> 19) + 4096
        start = jnp.minimum((lo >> 3) << 3, ROWS - WIN)
        return pl.multiple_of(start, 8), (hi - start) // WIN

    @pl.loop(0, NBLK // UNROLL)
    def _(g):
        extra = 0
        parts = []
        for u in range(UNROLL):
            b = g * UNROLL + u
            start, more = bounds(b)
            parts.append((start, block(b, start, None)))
            extra = extra + more
        for start, part in parts:
            acc[pl.ds(start, WIN), :] += part

        @pl.when(extra > 0)
        def _():
            @pl.loop(0, UNROLL)
            def _(u):
                b = g * UNROLL + u
                start, more = bounds(b)

                @pl.loop(0, more)
                def _(n):
                    begin = start + (n + 1) * WIN
                    place = pl.multiple_of(jnp.minimum(begin, ROWS - WIN), 8)
                    acc[pl.ds(place, WIN), :] += block(b, place, begin)

    @pl.loop(0, CZ // 4)
    def _(step):
        rows = acc[pl.ds(pl.multiple_of(step * (4 * PLANE), 8), 4 * PLANE), :]
        both = jnp.dot(jnp.concatenate(pair_of(rows), axis=1), forth[...], preferred_element_type=F32)
        out[pl.ds(step * 4, 4)] = (both[:, :CY] + both[:, CY:]).reshape(4, PLANE, CY)


def deposit(count, zc, xc, yc, mass, forth):
    hbm = pl.BlockSpec(memory_space=pltpu.HBM)
    return pl.pallas_call(
        deposit_kernel,
        out_shape=jax.ShapeDtypeStruct((CZ, PLANE, CY), F32),
        in_specs=[pl.BlockSpec(memory_space=pltpu.SMEM)] + [hbm] * 5,
        out_specs=pl.BlockSpec(memory_space=pltpu.VMEM),
        scratch_shapes=[
            pltpu.VMEM((ROWS, CY), F32),
            pltpu.VMEM((128, 128), jnp.int32),
            pltpu.VMEM((128, 128), jnp.int32),
            pltpu.VMEM((128, 128), jnp.int32),
            pltpu.VMEM((1, 1, SLOTS), BF16),
            pltpu.VMEM((2 * CY, 2 * CY), BF16),
            pltpu.VMEM((128, 128), F32),
            pltpu.VMEM((128, 128), jnp.int32),
            pltpu.VMEM((128, 128), jnp.int32),
            pltpu.VMEM((2, 8, 128), jnp.int32),
            pltpu.SMEM((2, 8, 128), jnp.int32),
            pltpu.SemaphoreType.DMA((6,)),
        ],
        compiler_params=pltpu.CompilerParams(vmem_limit_bytes=12 << 20),
        name="deposit",
    )(count, zc, xc, yc, mass, forth)


CHUNK = 64
CHUNKS = CX // CHUNK
SPAN = CHUNK + 16
ORDER = (1, 2, 0, 3)
PARTS = ((64, 96), (160, 64), (8, 56), (224, 56))


def sweep(src, at, dst, lo, hi, unroll, center, ratio, x_live):
    @pl.loop(0, (hi - lo) // unroll)
    def _(step):
        for n in range(SPAN // 8):
            r = at + 8 * n
            for u in range(unroll):
                z = lo + step * unroll + u
                along_z = src[z - 1, r : r + 8, :] + src[z + 1, r : r + 8, :]
                along_x = src[z, r - 1 : r + 7, :] + src[z, r + 1 : r + 9, :]
                new = src[z, r : r + 8, :] * center + along_x * ratio + along_z
                if n in x_live:
                    new = new * x_live[n]
                dst[z, 8 + 8 * n : 16 + 8 * n, :] = new


def back_to_cells(src, dst, grad, back, back_low, scale):
    rows = 6 * SPAN

    @pl.loop(0, (CZ + 2) // 6)
    def _(step):
        z = step * 6
        top, rest = pair_of(src[pl.ds(z + HALO - 1, 6), 8 : 8 + SPAN, :].reshape(rows, CY) * scale)
        mixed = jnp.dot(jnp.concatenate([top, rest], axis=1), back[...], preferred_element_type=F32)
        mixed = (mixed + jnp.dot(top, back_low[...], preferred_element_type=F32)).reshape(6, SPAN, 2 * CY)
        dst[pl.ds(z + HALO - 1, 6), 8 : 8 + SPAN, :] = mixed[:, :, :CY]
        grad[pl.ds(z, 6)] = mixed[:, 8 : 8 + CHUNK, CY:]


def gradient(src, grad, rise_d, rise_g):
    for n in range(CHUNK // 8):
        r, at = 16 + 8 * n, slice(8 * n, 8 * n + 8)
        for z in range(CZ):
            here = src[z + HALO, r : r + 8, :]
            before = src[z + HALO - 1, r : r + 8, :]
            gz = src[z + HALO + 1, r : r + 8, :] - before
            gx = src[z + HALO, r + 1 : r + 9, :] - src[z + HALO, r - 1 : r + 7, :]
            gy = grad[z + 1, at, :]
            square = (gz * gz + gx * gx) * 0.25 + gy * gy
            if z == 0:
                rise_g[0, at, :] = square
            else:
                rise_g[z, at, :] = square - last
                rise_d[z, at, :] = here - before
            last = square
        rise_g[CZ, at, :] = last


def render(dens, rise_d, rise_g, out, slope, shift, scale):
    rows = slice(16, 16 + CHUNK)
    over = 1.0 - scale
    sum_d, sum_g = dens[HALO, rows, :], rise_g[0]
    for z in range(CZ):
        t = jnp.tanh(dens[z + HALO, rows, :] * slope + shift)
        through = over - t * scale
        if z == 0:
            keep = through
        else:
            sum_d = sum_d + keep * rise_d[z]
            sum_g = sum_g + keep * rise_g[z]
            keep = keep * through
    out[0] = sum_d - keep * dens[HALO + CZ - 1, rows, :]
    out[1] = sum_g - keep * rise_g[CZ]
    out[2] = keep


def image_kernel(
    dif_h, tfc_h, tfs_h, tfo_h, shade_h, tint_h, cosine_h, back_h, low_h, ext, out,
    one, ta, tb, left, right, grad, rise_d, rise_g, mine, came, whole,
    dif, tfc, tfs, tfo, shade, tint, cosine, back, back_low,
    load_sem, local_sem, side_send, side_recv, halo_send, halo_recv, pair_send, pair_recv, far_send, far_recv,
):
    depth, cols = lax.axis_index("depth"), lax.axis_index("cols")
    nd, nc = lax.axis_size("depth"), lax.axis_size("cols")
    core, chip = depth % 2, depth // 2
    chips = nd // 2
    partner = (depth + 1 - 2 * core, cols)

    def beside(dz, dx):
        return ((depth + dz + nd) % nd, (cols + dx + nc) % nc)

    barrier = pltpu.get_barrier_semaphore()
    friends = [beside(-1, 0), beside(1, 0), beside(0, -1), beside(0, 1)]
    friends += [((depth + 2 * n) % nd, cols) for n in range(1, chips)]
    for friend in friends:
        pl.semaphore_signal(barrier, inc=1, device_id=friend, device_id_type=MESH)
    pairs = (
        (dif_h, dif), (tfc_h, tfc), (tfs_h, tfs), (tfo_h, tfo), (shade_h, shade), (tint_h, tint),
        (cosine_h, cosine), (back_h, back), (low_h, back_low),
    )
    loads = [pltpu.make_async_copy(source, target, load_sem.at[n]) for n, (source, target) in enumerate(pairs)]
    inner = pltpu.make_async_copy(ext, one.at[pl.ds(HALO, CZ)], local_sem)
    inner.start()
    for load in loads:
        load.start()
    zeros = jnp.zeros((8, CY), F32)

    @pl.loop(0, DEEP)
    def _(z):
        for t in (ta, tb):
            t[z, 0:8, :] = zeros
            t[z, 8 + SPAN : 16 + SPAN, :] = zeros

    for z in (*range(HALO), *range(HALO + CZ, DEEP)):
        one[z, 0:8, :] = zeros
        one[z, 280:288, :] = zeros
    pl.semaphore_wait(barrier, len(friends))

    planes = {1: (CZ - HALO, 0, HALO), -1: (0, HALO + CZ, HALO)}

    def copy_to(source, target, send, recv, device):
        copy = pltpu.make_async_remote_copy(
            src_ref=source, dst_ref=target, send_sem=send, recv_sem=recv, device_id=device, device_id_type=MESH
        )
        copy.start()
        return copy

    halos, sides = [], []

    def send_side(n, source, begin, count, at):
        for m, dx, target in ((0, 1, left), (1, -1, right)):
            sides.append(
                copy_to(
                    source.at[pl.ds(begin, count), pl.ds(264 if dx == 1 else 8, 16)], target.at[pl.ds(at, count)],
                    side_send.at[n, m], side_recv.at[n, m], beside(0, dx),
                )
            )

    for step, (begin, rows) in enumerate(PARTS):
        for n, dz in enumerate((-1, 1)):
            src, dst, count = planes[dz]
            halos.append(
                copy_to(
                    ext.at[pl.ds(src, count), pl.ds(begin, rows)], one.at[pl.ds(dst, count), pl.ds(begin, rows)],
                    halo_send.at[step, n], halo_recv.at[step, n], beside(dz, 0),
                )
            )
    send_side(0, ext, 0, CZ, HALO)
    inner.wait()
    for load in loads:
        load.wait()

    has_left = jnp.where(cols > 0, 1.0, 0.0)
    has_right = jnp.where(cols < nc - 1, 1.0, 0.0)
    d0, d1, d2 = dif[0], dif[1], dif[2]
    along = jnp.full((8, CY), d0, F32)
    center = (cosine[...] * d2 + (1.0 - 2.0 * (d0 + d1 + d2))) / along
    ratio = jnp.full((8, CY), d1, F32) / along
    square = d0 * d0

    def clear(ref, first, begin, rows):
        @pl.when(depth == 0)
        def _():
            for z in range(first, HALO):
                ref[z, begin : begin + rows, :] = jnp.zeros((rows, CY), F32)

        @pl.when(depth == nd - 1)
        def _():
            for z in range(HALO + CZ, DEEP - first):
                ref[z, begin : begin + rows, :] = jnp.zeros((rows, CY), F32)

    def arrive(step):
        for halo in halos[2 * step : 2 * step + 2]:
            halo.wait()

    def draw(chunk, own):
        @pl.loop(0, chips)
        def _(j):
            k = 2 * ((chip + j + 2) % chips) + (core if own else 1 - core)
            sharp = 0.5 * tfs[k]
            out_ref = mine.at[chunk, j + (chips if own else 0)]
            render(ta, rise_d, rise_g, out_ref, sharp, -sharp * tfc[k], 0.5 * tfo[k])

    swaps, sends = {}, []

    def combine(chunk):
        swaps[chunk].wait_recv()
        for j in range(chips):
            i = (chip + j + 2) % chips
            held = mine.at[chunk, chips + j]
            place = whole.at[chip, chunk] if j == 2 else held
            for n in range(CHUNK // 32):
                at = pl.ds(32 * n, 32)
                first = [jnp.where(core == 0, held[q, at, :], came[chunk, j, q, at, :]) for q in range(3)]
                then = [jnp.where(core == 0, came[chunk, j, q, at, :], held[q, at, :]) for q in range(3)]
                place[0, at, :] = first[0] + first[2] * then[0]
                place[1, at, :] = first[1] + first[2] * then[1]
                place[2, at, :] = first[2] * then[2]
            if j != 2:
                m = j - j // 3
                sends.append(
                    copy_to(
                        held, whole.at[chip, chunk], far_send.at[chunk, m], far_recv.at[chunk, m],
                        (2 * i + core, cols),
                    )
                )

    for step in range(CHUNKS):
        chunk = ORDER[step]
        if step < 2:
            arrive(step)
            clear(one, 0, *PARTS[step])
        if step == 2:
            for side in sides:
                side.wait()

            @pl.loop(0, DEEP)
            def _(z):
                one[z, 8:16, :] = (one[z, 8:16, :] + left[z, 0:8, :]) * has_left
                one[z, 16:24, :] = one[z, 16:24, :] + left[z, 8:16, :] * has_left
                one[z, 264:272, :] = one[z, 264:272, :] + right[z, 0:8, :] * has_right
                one[z, 272:280, :] = (one[z, 272:280, :] + right[z, 8:16, :]) * has_right

            clear(one, 0, *PARTS[2])
            clear(one, 0, *PARTS[3])
        x_live = {0: has_left} if chunk == 0 else {SPAN // 8 - 1: has_right} if chunk == CHUNKS - 1 else {}
        sweep(one, 8 + CHUNK * chunk, ta, 1, DEEP - 1, 8, center, ratio, x_live)
        clear(ta, 1, 8, SPAN)
        sweep(ta, 8, tb, 2, DEEP - 2, 11, center, ratio, x_live)
        clear(tb, 2, 8, SPAN)
        if step:
            combine(ORDER[step - 1])
        sweep(tb, 8, ta, 3, DEEP - 3, 10, center, ratio, x_live)
        clear(ta, 3, 8, SPAN)
        sweep(ta, 8, tb, 4, DEEP - 4, 9, center, ratio, x_live)
        clear(tb, 4, 8, SPAN)
        if step == 1:
            arrive(2)
            arrive(3)
            send_side(1, one, 0, HALO, 0)
            send_side(2, one, HALO + CZ, HALO, HALO + CZ)
        back_to_cells(tb, ta, grad, back, back_low, square * square)
        gradient(ta, grad, rise_d, rise_g)
        draw(chunk, False)
        swaps[chunk] = copy_to(
            mine.at[chunk, pl.ds(0, chips)], came.at[chunk], pair_send.at[chunk], pair_recv.at[chunk], partner
        )
        draw(chunk, True)
    combine(ORDER[-1])

    color = [tint[q, depth] for q in range(3)]
    shading = shade[depth]
    for step in range(CHUNKS):
        for send in sends[3 * step : 3 * step + 3]:
            send.wait()
        chunk = ORDER[step]
        for n in range(CHUNK // 32):
            at = pl.ds(32 * n, 32)
            to = pl.ds(CHUNK * chunk + 32 * n, 32)
            sum_d, sum_g, keep = (whole[chips - 1, chunk, q, at, :] for q in range(3))
            for i in range(chips - 2, -1, -1):
                near = whole[i, chunk, 2, at, :]
                sum_d = whole[i, chunk, 0, at, :] + near * sum_d
                sum_g = whole[i, chunk, 1, at, :] + near * sum_g
                keep = near * keep
            for q in range(3):
                out[q, to, :] = sum_d * color[q] + sum_g * shading
            out[3, to, :] = keep
    for chunk in ORDER:
        swaps[chunk].wait_send()


def image(*operands):
    tall = pltpu.VMEM((DEEP, SPAN + 16, CY), F32)
    strip = pltpu.VMEM((DEEP, 16, CY), F32)
    return pl.pallas_call(
        image_kernel,
        out_shape=jax.ShapeDtypeStruct((4, CX, CY), F32),
        in_specs=[pl.BlockSpec(memory_space=pl.ANY)] * 10,
        out_specs=pl.BlockSpec(memory_space=pltpu.VMEM),
        scratch_shapes=[
            pltpu.VMEM((DEEP, PLANE, CY), F32),
            tall,
            tall,
            strip,
            strip,
            pltpu.VMEM((CZ + 2, CHUNK, CY), F32),
            pltpu.VMEM((CZ, CHUNK, CY), F32),
            pltpu.VMEM((CZ + 1, CHUNK, CY), F32),
            pltpu.VMEM((CHUNKS, TFS, 3, CHUNK, CY), F32),
            pltpu.VMEM((CHUNKS, 4, 3, CHUNK, CY), F32),
            pltpu.VMEM((4, CHUNKS, 3, CHUNK, CY), F32),
            pltpu.SMEM((3,), F32),
            *[pltpu.SMEM((TFS,), F32)] * 4,
            pltpu.SMEM((3, TFS), F32),
            pltpu.VMEM((8, CY), F32),
            pltpu.VMEM((2 * CY, 2 * CY), BF16),
            pltpu.VMEM((CY, 2 * CY), BF16),
            pltpu.SemaphoreType.DMA((9,)),
            pltpu.SemaphoreType.DMA,
            pltpu.SemaphoreType.DMA((3, 2)),
            pltpu.SemaphoreType.DMA((3, 2)),
            pltpu.SemaphoreType.DMA((CHUNKS, 2)),
            pltpu.SemaphoreType.DMA((CHUNKS, 2)),
            pltpu.SemaphoreType.DMA((CHUNKS,)),
            pltpu.SemaphoreType.DMA((CHUNKS,)),
            pltpu.SemaphoreType.DMA((CHUNKS, 3)),
            pltpu.SemaphoreType.DMA((CHUNKS, 3)),
        ],
        compiler_params=pltpu.CompilerParams(collective_id=0, has_side_effects=True, vmem_limit_bytes=32 << 20),
        name="image",
    )(*operands)


def shards(depth_cell, column_cell, row_cell, mass, counts, diffusion, tf_center, tf_sharp, tf_opacity, tf_shade, tf_color):
    forth, back, back_low, cosine = (jnp.asarray(table) for table in tables())
    cells = [cell.reshape(128, 128) for cell in (depth_cell, column_cell, row_cell)]
    extended = deposit(counts, *cells, mass, forth)
    return image(
        diffusion, tf_center, tf_sharp, tf_opacity, tf_shade, tf_color.T, cosine, back, back_low, extended
    )


def solution(mesh):
    brick = P("depth", "cols", None)
    placed = (brick,) * 4 + (P("depth", "cols"),) + (P(),) * 6
    return jax.shard_map(shards, mesh=mesh, in_specs=placed, out_specs=brick, check_vma=False)
```

```python
import functools

import jax
import jax.numpy as jnp
import numpy as np
from jax import lax
from jax.experimental import pallas as pl
from jax.experimental.pallas import tpu as pltpu
from jax.sharding import PartitionSpec as P

CZ, CX, CY, RIM = 16, 256, 128, 4
SMOOTH, TFS = 4, 8
HALO = SMOOTH + 1
DEEP = CZ + 2 * HALO
PLANE = 288
XO = 16
ROWS = CZ * PLANE
WIN = 112
UNROLL = 8
SLOTS = 16384
NBLK = SLOTS // 256
MESH = pl.DeviceIdType.MESH
F32, BF16 = jnp.float32, jnp.bfloat16


def split(matrix):
    top = matrix.astype(BF16)
    return top, (matrix - top.astype(np.float64)).astype(BF16)


def tables():
    n = np.arange(1, CY + 1, dtype=np.float64)
    sine = np.sqrt(2.0 / (CY + 1)) * np.sin(np.pi * np.outer(n, n) / (CY + 1))
    slope = 0.5 * (np.eye(CY, k=-1) - np.eye(CY, k=1))
    s_top, s_low = split(sine)
    b_top, b_low = split(np.concatenate([sine, sine @ slope], axis=1))
    cosine = np.broadcast_to(2.0 * np.cos(np.pi * n / (CY + 1)), (8, CY)).astype(np.float32)
    forth = np.block([[s_top, s_low], [s_top, np.zeros_like(s_low)]])
    return forth, np.concatenate([b_top, b_top]), b_low, cosine


def pair_of(value):
    top = value.astype(BF16)
    return top, (value - top.astype(F32)).astype(BF16)


def exchange(x, stride, axis, bit):
    size = x.shape[axis]
    up = pltpu.roll(x, size - stride, axis)
    down = up if 2 * stride == size else pltpu.roll(x, stride, axis)
    return jnp.where(bit, jnp.maximum(x, down), jnp.minimum(x, up))


def bitonic(vs):
    lane = lax.broadcasted_iota(jnp.int32, (8, 128), 1)
    sub = lax.broadcasted_iota(jnp.int32, (8, 128), 0)
    bits = {j: (sub >> (j - 4)) & 1 if j < 7 else (lane >> (j - 7)) & 1 for j in range(4, 14)}
    hot = {j: bits[j] == 1 for j in bits}
    neg = {j: -bits[j] for j in bits}

    def flips(j, i):
        if j == 0 or j == 14:
            return 0
        return -((i >> j) & 1) if j < 4 else neg[j]

    for k in range(1, 15):
        out = []
        for i, v in enumerate(vs):
            a, b = flips(k - 1, i), flips(k, i)
            if isinstance(a, int) and isinstance(b, int):
                out.append(~v if a != b else v)
            else:
                out.append(v ^ (a ^ b))
        vs = out
        for j in range(k - 1, 6 if k == 14 else -1, -1):
            if j >= 7:
                vs = [exchange(v, 1 << (j - 7), 1, hot[j]) for v in vs]
            elif j >= 4:
                vs = [exchange(v, 1 << (j - 4), 0, hot[j]) for v in vs]
            else:
                out = list(vs)
                for i in range(16):
                    p = i ^ (1 << j)
                    if i < p:
                        out[i] = jnp.minimum(vs[i], vs[p])
                        out[p] = jnp.maximum(vs[i], vs[p])
                vs = out
    return vs


def deposit_kernel(count, zh, xh, yh, mh, fh, out, acc, zc, xc, yc, mass, forth, wide, raw, tidy, range_of, ends, sem):
    loads = [
        pltpu.make_async_copy(source, target, sem.at[n])
        for n, (source, target) in enumerate(((mh, mass), (zh, zc), (xh, xc), (yh, yc), (fh, forth)))
    ]
    for load in loads:
        load.start()
    zeros = jnp.zeros((PLANE, 128), F32)

    @pl.loop(0, CZ)
    def _(z):
        acc[pl.ds(pl.multiple_of(z * PLANE, 8), PLANE), :] = zeros

    loads[0].wait()
    for i in range(128):
        wide[i : i + 1, :] = mass[0, 0:1, 128 * i : 128 * i + 128].astype(F32)
    for load in loads[1:]:
        load.wait()
    slot = 128 * lax.broadcasted_iota(jnp.int32, (8, 128), 0) + lax.broadcasted_iota(jnp.int32, (8, 128), 1)
    live = count[0, 0]
    keys = []
    for i in range(16):
        at = pl.ds(8 * i, 8)
        weight = jnp.where(slot + 1024 * i < live, wide[at, :] * 64.0, 0.0).astype(jnp.int32)
        row = zc[at, :] * PLANE + xc[at, :] + (XO - RIM - 4096)
        keys.append((row << 19) | (yc[at, :] << 12) | weight)
    keys = bitonic(keys)
    range_of[0] = jnp.broadcast_to(jnp.min(functools.reduce(jnp.minimum, keys), axis=0, keepdims=True), (8, 128))
    range_of[1] = jnp.broadcast_to(jnp.max(functools.reduce(jnp.maximum, keys), axis=0, keepdims=True), (8, 128))
    found = pltpu.make_async_copy(range_of, ends, sem.at[5])
    found.start()
    for i in range(16):
        raw[8 * i : 8 * i + 8, :] = keys[i]
    tidy[...] = raw[...].T
    found.wait()
    ys = lax.broadcasted_iota(jnp.int32, (128, 128), 0)
    ws = lax.broadcasted_iota(jnp.int32, (WIN, 128), 0)

    def block(b, start, begin):
        hots, y_hots = [], []
        for half in range(2):
            key = tidy[pl.ds(2 * b + half, 1), :]
            row = (key >> 19) + 4096
            if begin is not None:
                row = jnp.where(row >= begin, row, -1)
            hots.append(jnp.where(ws == row - start, 1.0, 0.0).astype(BF16))
            weight = (key & 4095).astype(F32) * (1.0 / 64.0)
            y_hots.append(jnp.where(ys == ((key >> 12) & 127), weight, 0.0).astype(BF16))
        hot, y_hot = jnp.concatenate(hots, axis=1), jnp.concatenate(y_hots, axis=1)
        return lax.dot_general(hot, y_hot, (((1,), (1,)), ((), ())), preferred_element_type=F32)

    def bounds(b):
        lo = (ends[0, 0, 2 * b] >> 19) + 4096
        hi = (ends[1, 0, 2 * b + 1] >> 19) + 4096
        start = jnp.minimum((lo >> 3) << 3, ROWS - WIN)
        return pl.multiple_of(start, 8), (hi - start) // WIN

    @pl.loop(0, NBLK // UNROLL)
    def _(g):
        extra = 0
        parts = []
        for u in range(UNROLL):
            b = g * UNROLL + u
            start, more = bounds(b)
            parts.append((start, block(b, start, None)))
            extra = extra + more
        for start, part in parts:
            acc[pl.ds(start, WIN), :] += part

        @pl.when(extra > 0)
        def _():
            @pl.loop(0, UNROLL)
            def _(u):
                b = g * UNROLL + u
                start, more = bounds(b)

                @pl.loop(0, more)
                def _(n):
                    begin = start + (n + 1) * WIN
                    place = pl.multiple_of(jnp.minimum(begin, ROWS - WIN), 8)
                    acc[pl.ds(place, WIN), :] += block(b, place, begin)

    @pl.loop(0, CZ // 4)
    def _(step):
        rows = acc[pl.ds(pl.multiple_of(step * (4 * PLANE), 8), 4 * PLANE), :]
        both = jnp.dot(jnp.concatenate(pair_of(rows), axis=1), forth[...], preferred_element_type=F32)
        out[pl.ds(step * 4, 4)] = (both[:, :CY] + both[:, CY:]).reshape(4, PLANE, CY)


def deposit(count, zc, xc, yc, mass, forth):
    hbm = pl.BlockSpec(memory_space=pltpu.HBM)
    return pl.pallas_call(
        deposit_kernel,
        out_shape=jax.ShapeDtypeStruct((CZ, PLANE, CY), F32),
        in_specs=[pl.BlockSpec(memory_space=pltpu.SMEM)] + [hbm] * 5,
        out_specs=pl.BlockSpec(memory_space=pltpu.VMEM),
        scratch_shapes=[
            pltpu.VMEM((ROWS, CY), F32),
            pltpu.VMEM((128, 128), jnp.int32),
            pltpu.VMEM((128, 128), jnp.int32),
            pltpu.VMEM((128, 128), jnp.int32),
            pltpu.VMEM((1, 1, SLOTS), BF16),
            pltpu.VMEM((2 * CY, 2 * CY), BF16),
            pltpu.VMEM((128, 128), F32),
            pltpu.VMEM((128, 128), jnp.int32),
            pltpu.VMEM((128, 128), jnp.int32),
            pltpu.VMEM((2, 8, 128), jnp.int32),
            pltpu.SMEM((2, 8, 128), jnp.int32),
            pltpu.SemaphoreType.DMA((6,)),
        ],
        compiler_params=pltpu.CompilerParams(vmem_limit_bytes=12 << 20),
        name="deposit",
    )(count, zc, xc, yc, mass, forth)


CHUNK = 64
CHUNKS = CX // CHUNK
SPAN = CHUNK + 16
ORDER = (1, 2, 0, 3)
PARTS = ((64, 96), (160, 64), (8, 56), (224, 56))


def sweep(src, at, dst, lo, hi, unroll, center, ratio, x_live):
    @pl.loop(0, (hi - lo) // unroll)
    def _(step):
        for n in range(SPAN // 8):
            r = at + 8 * n
            for u in range(unroll):
                z = lo + step * unroll + u
                along_z = src[z - 1, r : r + 8, :] + src[z + 1, r : r + 8, :]
                along_x = src[z, r - 1 : r + 7, :] + src[z, r + 1 : r + 9, :]
                new = src[z, r : r + 8, :] * center + along_x * ratio + along_z
                if n in x_live:
                    new = new * x_live[n]
                dst[z, 8 + 8 * n : 16 + 8 * n, :] = new


def back_to_cells(src, dst, grad, back, back_low, scale):
    rows = 6 * SPAN

    @pl.loop(0, (CZ + 2) // 6)
    def _(step):
        z = step * 6
        top, rest = pair_of(src[pl.ds(z + HALO - 1, 6), 8 : 8 + SPAN, :].reshape(rows, CY) * scale)
        mixed = jnp.dot(jnp.concatenate([top, rest], axis=1), back[...], preferred_element_type=F32)
        mixed = (mixed + jnp.dot(top, back_low[...], preferred_element_type=F32)).reshape(6, SPAN, 2 * CY)
        dst[pl.ds(z + HALO - 1, 6), 8 : 8 + SPAN, :] = mixed[:, :, :CY]
        grad[pl.ds(z, 6)] = mixed[:, 8 : 8 + CHUNK, CY:]


def gradient(src, grad, rise_d, rise_g):
    for n in range(CHUNK // 8):
        r, at = 16 + 8 * n, slice(8 * n, 8 * n + 8)
        for z in range(CZ):
            here = src[z + HALO, r : r + 8, :]
            before = src[z + HALO - 1, r : r + 8, :]
            gz = src[z + HALO + 1, r : r + 8, :] - before
            gx = src[z + HALO, r + 1 : r + 9, :] - src[z + HALO, r - 1 : r + 7, :]
            gy = grad[z + 1, at, :]
            square = (gz * gz + gx * gx) * 0.25 + gy * gy
            if z == 0:
                rise_g[0, at, :] = square
            else:
                rise_g[z, at, :] = square - last
                rise_d[z, at, :] = here - before
            last = square
        rise_g[CZ, at, :] = last


def render(dens, rise_d, rise_g, out, slope, shift, scale):
    rows = slice(16, 16 + CHUNK)
    over = 1.0 - scale
    sum_d, sum_g = dens[HALO, rows, :], rise_g[0]
    for z in range(CZ):
        t = jnp.tanh(dens[z + HALO, rows, :] * slope + shift)
        through = over - t * scale
        if z == 0:
            keep = through
        else:
            sum_d = sum_d + keep * rise_d[z]
            sum_g = sum_g + keep * rise_g[z]
            keep = keep * through
    out[0] = sum_d - keep * dens[HALO + CZ - 1, rows, :]
    out[1] = sum_g - keep * rise_g[CZ]
    out[2] = keep


def image_kernel(
    dif_h, tfc_h, tfs_h, tfo_h, shade_h, tint_h, cosine_h, back_h, low_h, ext, out,
    one, ta, tb, left, right, grad, rise_d, rise_g, mine, came, whole,
    dif, tfc, tfs, tfo, shade, tint, cosine, back, back_low,
    load_sem, local_sem, side_send, side_recv, halo_send, halo_recv, pair_send, pair_recv, far_send, far_recv,
):
    depth, cols = lax.axis_index("depth"), lax.axis_index("cols")
    nd, nc = lax.axis_size("depth"), lax.axis_size("cols")
    core, chip = depth % 2, depth // 2
    chips = nd // 2
    partner = (depth + 1 - 2 * core, cols)

    exists = {(-1, 0): depth > 0, (1, 0): depth < nd - 1, (0, -1): cols > 0, (0, 1): cols < nc - 1}
    barrier = pltpu.get_barrier_semaphore()

    def greet(device):
        pl.semaphore_signal(barrier, inc=1, device_id=device, device_id_type=MESH)

    for dz, dx in exists:
        pl.when(exists[dz, dx])(functools.partial(greet, (depth + dz, cols + dx)))
    for n in range(1, chips):
        greet(((depth + 2 * n) % nd, cols))
    pairs = (
        (dif_h, dif), (tfc_h, tfc), (tfs_h, tfs), (tfo_h, tfo), (shade_h, shade), (tint_h, tint),
        (cosine_h, cosine), (back_h, back), (low_h, back_low),
    )
    loads = [pltpu.make_async_copy(source, target, load_sem.at[n]) for n, (source, target) in enumerate(pairs)]
    inner = pltpu.make_async_copy(ext, one.at[pl.ds(HALO, CZ)], local_sem)
    inner.start()
    for load in loads:
        load.start()
    zeros = jnp.zeros((8, CY), F32)

    @pl.loop(0, DEEP)
    def _(z):
        for t in (ta, tb):
            t[z, 0:8, :] = zeros
            t[z, 8 + SPAN : 16 + SPAN, :] = zeros

    for z in (*range(HALO), *range(HALO + CZ, DEEP)):
        one[z, 0:8, :] = zeros
        one[z, 280:288, :] = zeros

    def clear(ref, first, begin, rows):
        @pl.when(depth == 0)
        def _():
            for z in range(first, HALO):
                ref[z, begin : begin + rows, :] = jnp.zeros((rows, CY), F32)

        @pl.when(depth == nd - 1)
        def _():
            for z in range(HALO + CZ, DEEP - first):
                ref[z, begin : begin + rows, :] = jnp.zeros((rows, CY), F32)

    clear(one, 0, 8, 272)

    @pl.when(cols == 0)
    def _():
        left[...] = jnp.zeros((DEEP, 16, CY), F32)

    @pl.when(cols == nc - 1)
    def _():
        right[...] = jnp.zeros((DEEP, 16, CY), F32)

    pl.semaphore_wait(barrier, sum(near.astype(jnp.int32) for near in exists.values()) + chips - 1)

    planes = {1: (CZ - HALO, 0, HALO), -1: (0, HALO + CZ, HALO)}

    def copy_of(source, target, send, recv, device):
        return pltpu.make_async_remote_copy(
            src_ref=source, dst_ref=target, send_sem=send, recv_sem=recv, device_id=device, device_id_type=MESH
        )

    def halo(step, dz, act):
        begin, rows = PARTS[step]
        src, dst, count = planes[dz]
        n = (1 + dz) // 2
        copy = copy_of(
            ext.at[pl.ds(src, count), pl.ds(begin, rows)], one.at[pl.ds(dst, count), pl.ds(begin, rows)],
            halo_send.at[step, n], halo_recv.at[step, n], (depth + dz, cols),
        )
        pl.when(exists[dz, 0])(lambda: getattr(copy, act)())

    def start_halo(step):
        for dz in (-1, 1):
            halo(step, dz, "start")

    def arrive(step):
        for dz in (-1, 1):
            halo(step, dz, "wait_send")
            begin, rows = PARTS[step]
            src, dst, count = planes[dz]
            n = (1 + dz) // 2
            copy = copy_of(
                ext.at[pl.ds(src, count), pl.ds(begin, rows)], one.at[pl.ds(dst, count), pl.ds(begin, rows)],
                halo_send.at[step, n], halo_recv.at[step, n], (depth - dz, cols),
            )
            pl.when(exists[-dz, 0])(copy.wait_recv)

    spots = ((0, CZ, HALO), (0, HALO, 0), (HALO + CZ, HALO, HALO + CZ))

    def side(n, act):
        begin, count, at = spots[n]
        source = one if n else ext
        for m, dx, target in ((0, 1, left), (1, -1, right)):
            copy = copy_of(
                source.at[pl.ds(begin, count), pl.ds(264 if dx == 1 else 8, 16)], target.at[pl.ds(at, count)],
                side_send.at[n, m], side_recv.at[n, m], (depth, cols + dx),
            )
            pl.when(exists[0, dx] if act != "wait_recv" else exists[0, -dx])(lambda: getattr(copy, act)())

    start_halo(0)
    side(0, "start")
    inner.wait()
    for load in loads:
        load.wait()

    has_left = jnp.where(cols > 0, 1.0, 0.0)
    has_right = jnp.where(cols < nc - 1, 1.0, 0.0)
    d0, d1, d2 = dif[0], dif[1], dif[2]
    along = jnp.full((8, CY), d0, F32)
    center = (cosine[...] * d2 + (1.0 - 2.0 * (d0 + d1 + d2))) / along
    ratio = jnp.full((8, CY), d1, F32) / along
    square = d0 * d0

    def draw(chunk, own):
        @pl.loop(0, chips)
        def _(j):
            k = 2 * ((chip + j + 2) % chips) + (core if own else 1 - core)
            sharp = 0.5 * tfs[k]
            out_ref = mine.at[chunk, j + (chips if own else 0)]
            render(ta, rise_d, rise_g, out_ref, sharp, -sharp * tfc[k], 0.5 * tfo[k])
            if not own:
                swap_of(chunk, j).start()

    def swap_of(chunk, j):
        return copy_of(
            mine.at[chunk, j], came.at[chunk, j], pair_send.at[chunk, j], pair_recv.at[chunk, j], partner
        )

    sends = []

    def combine(chunk):
        for j in (0, 1, 3, 2):
            swap_of(chunk, j).wait_recv()
            i = (chip + j + 2) % chips
            held = mine.at[chunk, chips + j]
            place = whole.at[chip, chunk] if j == 2 else held
            for n in range(CHUNK // 32):
                at = pl.ds(32 * n, 32)
                first = [jnp.where(core == 0, held[q, at, :], came[chunk, j, q, at, :]) for q in range(3)]
                then = [jnp.where(core == 0, came[chunk, j, q, at, :], held[q, at, :]) for q in range(3)]
                place[0, at, :] = first[0] + first[2] * then[0]
                place[1, at, :] = first[1] + first[2] * then[1]
                place[2, at, :] = first[2] * then[2]
            if j != 2:
                m = j - j // 3
                send = copy_of(
                    held, whole.at[chip, chunk], far_send.at[chunk, m], far_recv.at[chunk, m], (2 * i + core, cols)
                )
                send.start()
                sends.append(send)

    for step in range(CHUNKS):
        chunk = ORDER[step]
        if step < 2:
            arrive(step)
        if step == 0:
            for later in range(1, CHUNKS):
                start_halo(later)
        if step == 2:
            for n in range(3):
                side(n, "wait_send")
                side(n, "wait_recv")

            @pl.loop(0, DEEP)
            def _(z):
                one[z, 8:16, :] = (one[z, 8:16, :] + left[z, 0:8, :]) * has_left
                one[z, 16:24, :] = one[z, 16:24, :] + left[z, 8:16, :] * has_left
                one[z, 264:272, :] = one[z, 264:272, :] + right[z, 0:8, :] * has_right
                one[z, 272:280, :] = (one[z, 272:280, :] + right[z, 8:16, :]) * has_right
        x_live = {0: has_left} if chunk == 0 else {SPAN // 8 - 1: has_right} if chunk == CHUNKS - 1 else {}
        sweep(one, 8 + CHUNK * chunk, ta, 1, DEEP - 1, 8, center, ratio, x_live)
        clear(ta, 1, 8, SPAN)
        sweep(ta, 8, tb, 2, DEEP - 2, 11, center, ratio, x_live)
        clear(tb, 2, 8, SPAN)
        if step:
            combine(ORDER[step - 1])
        sweep(tb, 8, ta, 3, DEEP - 3, 10, center, ratio, x_live)
        clear(ta, 3, 8, SPAN)
        sweep(ta, 8, tb, 4, DEEP - 4, 9, center, ratio, x_live)
        clear(tb, 4, 8, SPAN)
        if step == 1:
            arrive(2)
            arrive(3)
            side(1, "start")
            side(2, "start")
        back_to_cells(tb, ta, grad, back, back_low, square * square)
        gradient(ta, grad, rise_d, rise_g)
        draw(chunk, False)
        draw(chunk, True)
    combine(ORDER[-1])

    color = [tint[q, depth] for q in range(3)]
    shading = shade[depth]
    for step in range(CHUNKS):
        for send in sends[3 * step : 3 * step + 3]:
            send.wait()
        chunk = ORDER[step]
        for n in range(CHUNK // 32):
            at = pl.ds(32 * n, 32)
            to = pl.ds(CHUNK * chunk + 32 * n, 32)
            sum_d, sum_g, keep = (whole[chips - 1, chunk, q, at, :] for q in range(3))
            for i in range(chips - 2, -1, -1):
                near = whole[i, chunk, 2, at, :]
                sum_d = whole[i, chunk, 0, at, :] + near * sum_d
                sum_g = whole[i, chunk, 1, at, :] + near * sum_g
                keep = near * keep
            for q in range(3):
                out[q, to, :] = sum_d * color[q] + sum_g * shading
            out[3, to, :] = keep
    for chunk in ORDER:
        for j in range(chips):
            swap_of(chunk, j).wait_send()


def image(*operands):
    tall = pltpu.VMEM((DEEP, SPAN + 16, CY), F32)
    strip = pltpu.VMEM((DEEP, 16, CY), F32)
    return pl.pallas_call(
        image_kernel,
        out_shape=jax.ShapeDtypeStruct((4, CX, CY), F32),
        in_specs=[pl.BlockSpec(memory_space=pl.ANY)] * 10,
        out_specs=pl.BlockSpec(memory_space=pltpu.VMEM),
        scratch_shapes=[
            pltpu.VMEM((DEEP, PLANE, CY), F32),
            tall,
            tall,
            strip,
            strip,
            pltpu.VMEM((CZ + 2, CHUNK, CY), F32),
            pltpu.VMEM((CZ, CHUNK, CY), F32),
            pltpu.VMEM((CZ + 1, CHUNK, CY), F32),
            pltpu.VMEM((CHUNKS, TFS, 3, CHUNK, CY), F32),
            pltpu.VMEM((CHUNKS, 4, 3, CHUNK, CY), F32),
            pltpu.VMEM((4, CHUNKS, 3, CHUNK, CY), F32),
            pltpu.SMEM((3,), F32),
            *[pltpu.SMEM((TFS,), F32)] * 4,
            pltpu.SMEM((3, TFS), F32),
            pltpu.VMEM((8, CY), F32),
            pltpu.VMEM((2 * CY, 2 * CY), BF16),
            pltpu.VMEM((CY, 2 * CY), BF16),
            pltpu.SemaphoreType.DMA((9,)),
            pltpu.SemaphoreType.DMA,
            pltpu.SemaphoreType.DMA((3, 2)),
            pltpu.SemaphoreType.DMA((3, 2)),
            pltpu.SemaphoreType.DMA((CHUNKS, 2)),
            pltpu.SemaphoreType.DMA((CHUNKS, 2)),
            pltpu.SemaphoreType.DMA((CHUNKS, 4)),
            pltpu.SemaphoreType.DMA((CHUNKS, 4)),
            pltpu.SemaphoreType.DMA((CHUNKS, 3)),
            pltpu.SemaphoreType.DMA((CHUNKS, 3)),
        ],
        compiler_params=pltpu.CompilerParams(collective_id=0, has_side_effects=True, vmem_limit_bytes=32 << 20),
        name="image",
    )(*operands)


def shards(depth_cell, column_cell, row_cell, mass, counts, diffusion, tf_center, tf_sharp, tf_opacity, tf_shade, tf_color):
    forth, back, back_low, cosine = (jnp.asarray(table) for table in tables())
    cells = [cell.reshape(128, 128) for cell in (depth_cell, column_cell, row_cell)]
    extended = deposit(counts, *(pltpu.with_memory_space_constraint(x, pltpu.HBM) for x in (*cells, mass, forth)))
    return image(
        diffusion, tf_center, tf_sharp, tf_opacity, tf_shade, tf_color.T, cosine, back, back_low, extended
    )


def solution(mesh):
    brick = P("depth", "cols", None)
    placed = (brick,) * 4 + (P("depth", "cols"),) + (P(),) * 6
    return jax.shard_map(shards, mesh=mesh, in_specs=placed, out_specs=brick, check_vma=False)
```

```python
import functools

import jax
import jax.numpy as jnp
import numpy as np
from jax import lax
from jax.experimental import pallas as pl
from jax.experimental.pallas import tpu as pltpu
from jax.sharding import PartitionSpec as P

CZ, CX, CY, RIM = 16, 256, 128, 4
SMOOTH, TFS = 4, 8
HALO = SMOOTH + 1
DEEP = CZ + 2 * HALO
PLANE = 288
XO = 16
ROWS = CZ * PLANE
WIN = 112
UNROLL = 8
SLOTS = 16384
NBLK = SLOTS // 256
MESH = pl.DeviceIdType.MESH
F32, BF16 = jnp.float32, jnp.bfloat16


def split(matrix):
    top = matrix.astype(BF16)
    return top, (matrix - top.astype(np.float64)).astype(BF16)


def tables():
    n = np.arange(1, CY + 1, dtype=np.float64)
    sine = np.sqrt(2.0 / (CY + 1)) * np.sin(np.pi * np.outer(n, n) / (CY + 1))
    slope = 0.5 * (np.eye(CY, k=-1) - np.eye(CY, k=1))
    s_top, s_low = split(sine)
    b_top, b_low = split(np.concatenate([sine, sine @ slope], axis=1))
    cosine = np.broadcast_to(2.0 * np.cos(np.pi * n / (CY + 1)), (8, CY)).astype(np.float32)
    forth = np.block([[s_top, s_low], [s_top, np.zeros_like(s_low)]])
    return forth, np.concatenate([b_top, b_top]), b_low, cosine


def pair_of(value):
    top = value.astype(BF16)
    return top, (value - top.astype(F32)).astype(BF16)


def exchange(x, stride, axis, bit):
    size = x.shape[axis]
    up = pltpu.roll(x, size - stride, axis)
    down = up if 2 * stride == size else pltpu.roll(x, stride, axis)
    return jnp.where(bit, jnp.maximum(x, down), jnp.minimum(x, up))


def bitonic(vs):
    lane = lax.broadcasted_iota(jnp.int32, (8, 128), 1)
    sub = lax.broadcasted_iota(jnp.int32, (8, 128), 0)
    bits = {j: (sub >> (j - 4)) & 1 if j < 7 else (lane >> (j - 7)) & 1 for j in range(4, 14)}
    hot = {j: bits[j] == 1 for j in bits}
    neg = {j: -bits[j] for j in bits}

    def flips(j, i):
        if j == 0 or j == 14:
            return 0
        return -((i >> j) & 1) if j < 4 else neg[j]

    for k in range(1, 15):
        out = []
        for i, v in enumerate(vs):
            a, b = flips(k - 1, i), flips(k, i)
            if isinstance(a, int) and isinstance(b, int):
                out.append(~v if a != b else v)
            else:
                out.append(v ^ (a ^ b))
        vs = out
        for j in range(k - 1, 6 if k == 14 else -1, -1):
            if j >= 7:
                vs = [exchange(v, 1 << (j - 7), 1, hot[j]) for v in vs]
            elif j >= 4:
                vs = [exchange(v, 1 << (j - 4), 0, hot[j]) for v in vs]
            else:
                out = list(vs)
                for i in range(16):
                    p = i ^ (1 << j)
                    if i < p:
                        out[i] = jnp.minimum(vs[i], vs[p])
                        out[p] = jnp.maximum(vs[i], vs[p])
                vs = out
    return vs


def deposit_kernel(count, zh, xh, yh, mh, fh, out, acc, zc, xc, yc, mass, forth, wide, raw, tidy, range_of, ends, sem):
    loads = [
        pltpu.make_async_copy(source, target, sem.at[n])
        for n, (source, target) in enumerate(((mh, mass), (zh, zc), (xh, xc), (yh, yc), (fh, forth)))
    ]
    for load in loads:
        load.start()
    zeros = jnp.zeros((PLANE, 128), F32)

    @pl.loop(0, CZ)
    def _(z):
        acc[pl.ds(pl.multiple_of(z * PLANE, 8), PLANE), :] = zeros

    loads[0].wait()
    for i in range(128):
        wide[i : i + 1, :] = mass[0, 0:1, 128 * i : 128 * i + 128].astype(F32)
    for load in loads[1:]:
        load.wait()
    slot = 128 * lax.broadcasted_iota(jnp.int32, (8, 128), 0) + lax.broadcasted_iota(jnp.int32, (8, 128), 1)
    live = count[0, 0]
    keys = []
    for i in range(16):
        at = pl.ds(8 * i, 8)
        weight = jnp.where(slot + 1024 * i < live, wide[at, :] * 64.0, 0.0).astype(jnp.int32)
        row = zc[at, :] * PLANE + xc[at, :] + (XO - RIM - 4096)
        keys.append((row << 19) | (yc[at, :] << 12) | weight)
    keys = bitonic(keys)
    range_of[0] = jnp.broadcast_to(jnp.min(functools.reduce(jnp.minimum, keys), axis=0, keepdims=True), (8, 128))
    range_of[1] = jnp.broadcast_to(jnp.max(functools.reduce(jnp.maximum, keys), axis=0, keepdims=True), (8, 128))
    found = pltpu.make_async_copy(range_of, ends, sem.at[5])
    found.start()
    for i in range(16):
        raw[8 * i : 8 * i + 8, :] = keys[i]
    tidy[...] = raw[...].T
    found.wait()
    ys = lax.broadcasted_iota(jnp.int32, (128, 128), 0)
    ws = lax.broadcasted_iota(jnp.int32, (WIN, 128), 0)

    def block(b, start, begin):
        hots, y_hots = [], []
        for half in range(2):
            key = tidy[pl.ds(2 * b + half, 1), :]
            row = (key >> 19) + 4096
            if begin is not None:
                row = jnp.where(row >= begin, row, -1)
            hots.append(jnp.where(ws == row - start, 1.0, 0.0).astype(BF16))
            weight = (key & 4095).astype(F32) * (1.0 / 64.0)
            y_hots.append(jnp.where(ys == ((key >> 12) & 127), weight, 0.0).astype(BF16))
        hot, y_hot = jnp.concatenate(hots, axis=1), jnp.concatenate(y_hots, axis=1)
        return lax.dot_general(hot, y_hot, (((1,), (1,)), ((), ())), preferred_element_type=F32)

    def bounds(b):
        lo = (ends[0, 0, 2 * b] >> 19) + 4096
        hi = (ends[1, 0, 2 * b + 1] >> 19) + 4096
        start = jnp.minimum((lo >> 3) << 3, ROWS - WIN)
        return pl.multiple_of(start, 8), (hi - start) // WIN

    @pl.loop(0, NBLK // UNROLL)
    def _(g):
        extra = 0
        parts = []
        for u in range(UNROLL):
            b = g * UNROLL + u
            start, more = bounds(b)
            parts.append((start, block(b, start, None)))
            extra = extra + more
        for start, part in parts:
            acc[pl.ds(start, WIN), :] += part

        @pl.when(extra > 0)
        def _():
            @pl.loop(0, UNROLL)
            def _(u):
                b = g * UNROLL + u
                start, more = bounds(b)

                @pl.loop(0, more)
                def _(n):
                    begin = start + (n + 1) * WIN
                    place = pl.multiple_of(jnp.minimum(begin, ROWS - WIN), 8)
                    acc[pl.ds(place, WIN), :] += block(b, place, begin)

    @pl.loop(0, CZ // 4)
    def _(step):
        rows = acc[pl.ds(pl.multiple_of(step * (4 * PLANE), 8), 4 * PLANE), :]
        both = jnp.dot(jnp.concatenate(pair_of(rows), axis=1), forth[...], preferred_element_type=F32)
        out[pl.ds(step * 4, 4)] = (both[:, :CY] + both[:, CY:]).reshape(4, PLANE, CY)


def deposit(count, zc, xc, yc, mass, forth):
    hbm = pl.BlockSpec(memory_space=pltpu.HBM)
    return pl.pallas_call(
        deposit_kernel,
        out_shape=jax.ShapeDtypeStruct((CZ, PLANE, CY), F32),
        in_specs=[pl.BlockSpec(memory_space=pltpu.SMEM)] + [hbm] * 5,
        out_specs=pl.BlockSpec(memory_space=pltpu.VMEM),
        scratch_shapes=[
            pltpu.VMEM((ROWS, CY), F32),
            pltpu.VMEM((128, 128), jnp.int32),
            pltpu.VMEM((128, 128), jnp.int32),
            pltpu.VMEM((128, 128), jnp.int32),
            pltpu.VMEM((1, 1, SLOTS), BF16),
            pltpu.VMEM((2 * CY, 2 * CY), BF16),
            pltpu.VMEM((128, 128), F32),
            pltpu.VMEM((128, 128), jnp.int32),
            pltpu.VMEM((128, 128), jnp.int32),
            pltpu.VMEM((2, 8, 128), jnp.int32),
            pltpu.SMEM((2, 8, 128), jnp.int32),
            pltpu.SemaphoreType.DMA((6,)),
        ],
        compiler_params=pltpu.CompilerParams(vmem_limit_bytes=12 << 20),
        name="deposit",
    )(count, zc, xc, yc, mass, forth)


CHUNK = 64
CHUNKS = CX // CHUNK
SPAN = CHUNK + 16
ORDER = (1, 2, 0, 3)
PARTS = ((64, 96), (160, 64), (8, 56), (224, 56))


def sweep(src, at, dst, lo, hi, unroll, center, ratio, x_live):
    @pl.loop(0, (hi - lo) // unroll)
    def _(step):
        for n in range(SPAN // 8):
            r = at + 8 * n
            for u in range(unroll):
                z = lo + step * unroll + u
                along_z = src[z - 1, r : r + 8, :] + src[z + 1, r : r + 8, :]
                along_x = src[z, r - 1 : r + 7, :] + src[z, r + 1 : r + 9, :]
                new = src[z, r : r + 8, :] * center + along_x * ratio + along_z
                if n in x_live:
                    new = new * x_live[n]
                dst[z, 8 + 8 * n : 16 + 8 * n, :] = new


def back_to_cells(src, dst, grad, back, back_low, scale):
    rows = 6 * SPAN

    @pl.loop(0, (CZ + 2) // 6)
    def _(step):
        z = step * 6
        top, rest = pair_of(src[pl.ds(z + HALO - 1, 6), 8 : 8 + SPAN, :].reshape(rows, CY) * scale)
        mixed = jnp.dot(jnp.concatenate([top, rest], axis=1), back[...], preferred_element_type=F32)
        mixed = (mixed + jnp.dot(top, back_low[...], preferred_element_type=F32)).reshape(6, SPAN, 2 * CY)
        dst[pl.ds(z + HALO - 1, 6), 8 : 8 + SPAN, :] = mixed[:, :, :CY]
        grad[pl.ds(z, 6)] = mixed[:, 8 : 8 + CHUNK, CY:]


def gradient(src, grad, rise_d, rise_g):
    for n in range(CHUNK // 8):
        r, at = 16 + 8 * n, slice(8 * n, 8 * n + 8)
        for z in range(CZ):
            here = src[z + HALO, r : r + 8, :]
            before = src[z + HALO - 1, r : r + 8, :]
            gz = src[z + HALO + 1, r : r + 8, :] - before
            gx = src[z + HALO, r + 1 : r + 9, :] - src[z + HALO, r - 1 : r + 7, :]
            gy = grad[z + 1, at, :]
            square = (gz * gz + gx * gx) * 0.25 + gy * gy
            if z == 0:
                rise_g[0, at, :] = square
            else:
                rise_g[z, at, :] = square - last
                rise_d[z, at, :] = here - before
            last = square
        rise_g[CZ, at, :] = last


def render(dens, rise_d, rise_g, out, slope, shift, scale):
    rows = slice(16, 16 + CHUNK)
    over = 1.0 - scale
    sum_d, sum_g = dens[HALO, rows, :], rise_g[0]
    for z in range(CZ):
        t = jnp.tanh(dens[z + HALO, rows, :] * slope + shift)
        through = over - t * scale
        if z == 0:
            keep = through
        else:
            sum_d = sum_d + keep * rise_d[z]
            sum_g = sum_g + keep * rise_g[z]
            keep = keep * through
    out[0] = sum_d - keep * dens[HALO + CZ - 1, rows, :]
    out[1] = sum_g - keep * rise_g[CZ]
    out[2] = keep


def image_kernel(
    dif_h, tfc_h, tfs_h, tfo_h, shade_h, tint_h, cosine_h, back_h, low_h, ext, out,
    one, ta, tb, left, right, grad, rise_d, rise_g, mine, came, whole,
    dif, tfc, tfs, tfo, shade, tint, cosine, back, back_low,
    load_sem, local_sem, side_send, side_recv, halo_send, halo_recv, pair_send, pair_recv, far_send, far_recv,
):
    depth, cols = lax.axis_index("depth"), lax.axis_index("cols")
    nd, nc = lax.axis_size("depth"), lax.axis_size("cols")
    core, chip = depth % 2, depth // 2
    chips = nd // 2
    partner = (depth + 1 - 2 * core, cols)

    exists = {(-1, 0): depth > 0, (1, 0): depth < nd - 1, (0, -1): cols > 0, (0, 1): cols < nc - 1}
    barrier = pltpu.get_barrier_semaphore()

    def greet(device):
        pl.semaphore_signal(barrier, inc=1, device_id=device, device_id_type=MESH)

    for dz, dx in exists:
        pl.when(exists[dz, dx])(functools.partial(greet, (depth + dz, cols + dx)))
    for n in range(1, chips):
        greet(((depth + 2 * n) % nd, cols))
    pairs = (
        (dif_h, dif), (tfc_h, tfc), (tfs_h, tfs), (tfo_h, tfo), (shade_h, shade), (tint_h, tint),
        (cosine_h, cosine), (back_h, back), (low_h, back_low),
    )
    loads = [pltpu.make_async_copy(source, target, load_sem.at[n]) for n, (source, target) in enumerate(pairs)]
    inner = pltpu.make_async_copy(ext, one.at[pl.ds(HALO, CZ)], local_sem)
    inner.start()
    for load in loads:
        load.start()
    zeros = jnp.zeros((8, CY), F32)

    @pl.loop(0, DEEP)
    def _(z):
        for t in (ta, tb):
            t[z, 0:8, :] = zeros
            t[z, 8 + SPAN : 16 + SPAN, :] = zeros

    for z in (*range(HALO), *range(HALO + CZ, DEEP)):
        one[z, 0:8, :] = zeros
        one[z, 280:288, :] = zeros

    def clear(ref, first, begin, rows):
        @pl.when(depth == 0)
        def _():
            for z in range(first, HALO):
                ref[z, begin : begin + rows, :] = jnp.zeros((rows, CY), F32)

        @pl.when(depth == nd - 1)
        def _():
            for z in range(HALO + CZ, DEEP - first):
                ref[z, begin : begin + rows, :] = jnp.zeros((rows, CY), F32)

    clear(one, 0, 8, 272)

    @pl.when(cols == 0)
    def _():
        left[...] = jnp.zeros((DEEP, 16, CY), F32)

    @pl.when(cols == nc - 1)
    def _():
        right[...] = jnp.zeros((DEEP, 16, CY), F32)

    pl.semaphore_wait(barrier, sum(near.astype(jnp.int32) for near in exists.values()) + chips - 1)

    planes = {1: (CZ - HALO, 0, HALO), -1: (0, HALO + CZ, HALO)}

    def copy_of(source, target, send, recv, device):
        return pltpu.make_async_remote_copy(
            src_ref=source, dst_ref=target, send_sem=send, recv_sem=recv, device_id=device, device_id_type=MESH
        )

    def halo(step, dz, act):
        begin, rows = PARTS[step]
        src, dst, count = planes[dz]
        n = (1 + dz) // 2
        copy = copy_of(
            ext.at[pl.ds(src, count), pl.ds(begin, rows)], one.at[pl.ds(dst, count), pl.ds(begin, rows)],
            halo_send.at[step, n], halo_recv.at[step, n], (depth + dz, cols),
        )
        pl.when(exists[dz, 0])(lambda: getattr(copy, act)())

    def start_halo(step):
        for dz in (-1, 1):
            halo(step, dz, "start")

    def arrive(step):
        for dz in (-1, 1):
            halo(step, dz, "wait_send")
            begin, rows = PARTS[step]
            src, dst, count = planes[dz]
            n = (1 + dz) // 2
            copy = copy_of(
                ext.at[pl.ds(src, count), pl.ds(begin, rows)], one.at[pl.ds(dst, count), pl.ds(begin, rows)],
                halo_send.at[step, n], halo_recv.at[step, n], (depth - dz, cols),
            )
            pl.when(exists[-dz, 0])(copy.wait_recv)

    spots = ((0, CZ, HALO), (0, HALO, 0), (HALO + CZ, HALO, HALO + CZ))

    def side(n, act):
        begin, count, at = spots[n]
        source = one if n else ext
        for m, dx, target in ((0, 1, left), (1, -1, right)):
            copy = copy_of(
                source.at[pl.ds(begin, count), pl.ds(264 if dx == 1 else 8, 16)], target.at[pl.ds(at, count)],
                side_send.at[n, m], side_recv.at[n, m], (depth, cols + dx),
            )
            pl.when(exists[0, dx] if act != "wait_recv" else exists[0, -dx])(lambda: getattr(copy, act)())

    start_halo(0)
    side(0, "start")
    for later in range(1, CHUNKS):
        start_halo(later)
    inner.wait()
    for load in loads:
        load.wait()

    has_left = jnp.where(cols > 0, 1.0, 0.0)
    has_right = jnp.where(cols < nc - 1, 1.0, 0.0)
    d0, d1, d2 = dif[0], dif[1], dif[2]
    along = jnp.full((8, CY), d0, F32)
    center = (cosine[...] * d2 + (1.0 - 2.0 * (d0 + d1 + d2))) / along
    ratio = jnp.full((8, CY), d1, F32) / along
    square = d0 * d0

    def draw(chunk, own):
        @pl.loop(0, chips)
        def _(j):
            k = 2 * ((chip + j + 2) % chips) + (core if own else 1 - core)
            sharp = 0.5 * tfs[k]
            out_ref = mine.at[chunk, j + (chips if own else 0)]
            render(ta, rise_d, rise_g, out_ref, sharp, -sharp * tfc[k], 0.5 * tfo[k])
            if not own:
                swap_of(chunk, j).start()

    def swap_of(chunk, j):
        return copy_of(
            mine.at[chunk, j], came.at[chunk, j], pair_send.at[chunk, j], pair_recv.at[chunk, j], partner
        )

    sends = []

    def combine(chunk):
        for j in (0, 1, 3, 2):
            swap_of(chunk, j).wait_recv()
            i = (chip + j + 2) % chips
            held = mine.at[chunk, chips + j]
            place = whole.at[chip, chunk] if j == 2 else held
            for n in range(CHUNK // 32):
                at = pl.ds(32 * n, 32)
                first = [jnp.where(core == 0, held[q, at, :], came[chunk, j, q, at, :]) for q in range(3)]
                then = [jnp.where(core == 0, came[chunk, j, q, at, :], held[q, at, :]) for q in range(3)]
                place[0, at, :] = first[0] + first[2] * then[0]
                place[1, at, :] = first[1] + first[2] * then[1]
                place[2, at, :] = first[2] * then[2]
            if j != 2:
                m = j - j // 3
                send = copy_of(
                    held, whole.at[chip, chunk], far_send.at[chunk, m], far_recv.at[chunk, m], (2 * i + core, cols)
                )
                send.start()
                sends.append(send)

    for step in range(CHUNKS):
        chunk = ORDER[step]
        if step < 2:
            arrive(step)
        if step == 2:
            for n in range(3):
                side(n, "wait_send")
                side(n, "wait_recv")

            @pl.loop(0, DEEP)
            def _(z):
                one[z, 8:16, :] = (one[z, 8:16, :] + left[z, 0:8, :]) * has_left
                one[z, 16:24, :] = one[z, 16:24, :] + left[z, 8:16, :] * has_left
                one[z, 264:272, :] = one[z, 264:272, :] + right[z, 0:8, :] * has_right
                one[z, 272:280, :] = (one[z, 272:280, :] + right[z, 8:16, :]) * has_right
        x_live = {0: has_left} if chunk == 0 else {SPAN // 8 - 1: has_right} if chunk == CHUNKS - 1 else {}
        sweep(one, 8 + CHUNK * chunk, ta, 1, DEEP - 1, 8, center, ratio, x_live)
        clear(ta, 1, 8, SPAN)
        sweep(ta, 8, tb, 2, DEEP - 2, 11, center, ratio, x_live)
        clear(tb, 2, 8, SPAN)
        if step:
            combine(ORDER[step - 1])
        sweep(tb, 8, ta, 3, DEEP - 3, 10, center, ratio, x_live)
        clear(ta, 3, 8, SPAN)
        sweep(ta, 8, tb, 4, DEEP - 4, 9, center, ratio, x_live)
        clear(tb, 4, 8, SPAN)
        if step == 1:
            arrive(2)
            arrive(3)
            side(1, "start")
            side(2, "start")
        back_to_cells(tb, ta, grad, back, back_low, square * square)
        gradient(ta, grad, rise_d, rise_g)
        draw(chunk, False)
        draw(chunk, True)
    combine(ORDER[-1])

    color = [tint[q, depth] for q in range(3)]
    shading = shade[depth]
    for step in range(CHUNKS):
        for send in sends[3 * step : 3 * step + 3]:
            send.wait()
        chunk = ORDER[step]
        for n in range(CHUNK // 32):
            at = pl.ds(32 * n, 32)
            to = pl.ds(CHUNK * chunk + 32 * n, 32)
            sum_d, sum_g, keep = (whole[chips - 1, chunk, q, at, :] for q in range(3))
            for i in range(chips - 2, -1, -1):
                near = whole[i, chunk, 2, at, :]
                sum_d = whole[i, chunk, 0, at, :] + near * sum_d
                sum_g = whole[i, chunk, 1, at, :] + near * sum_g
                keep = near * keep
            for q in range(3):
                out[q, to, :] = sum_d * color[q] + sum_g * shading
            out[3, to, :] = keep
    for chunk in ORDER:
        for j in range(chips):
            swap_of(chunk, j).wait_send()


def image(*operands):
    tall = pltpu.VMEM((DEEP, SPAN + 16, CY), F32)
    strip = pltpu.VMEM((DEEP, 16, CY), F32)
    return pl.pallas_call(
        image_kernel,
        out_shape=jax.ShapeDtypeStruct((4, CX, CY), F32),
        in_specs=[pl.BlockSpec(memory_space=pl.ANY)] * 10,
        out_specs=pl.BlockSpec(memory_space=pltpu.VMEM),
        scratch_shapes=[
            pltpu.VMEM((DEEP, PLANE, CY), F32),
            tall,
            tall,
            strip,
            strip,
            pltpu.VMEM((CZ + 2, CHUNK, CY), F32),
            pltpu.VMEM((CZ, CHUNK, CY), F32),
            pltpu.VMEM((CZ + 1, CHUNK, CY), F32),
            pltpu.VMEM((CHUNKS, TFS, 3, CHUNK, CY), F32),
            pltpu.VMEM((CHUNKS, 4, 3, CHUNK, CY), F32),
            pltpu.VMEM((4, CHUNKS, 3, CHUNK, CY), F32),
            pltpu.SMEM((3,), F32),
            *[pltpu.SMEM((TFS,), F32)] * 4,
            pltpu.SMEM((3, TFS), F32),
            pltpu.VMEM((8, CY), F32),
            pltpu.VMEM((2 * CY, 2 * CY), BF16),
            pltpu.VMEM((CY, 2 * CY), BF16),
            pltpu.SemaphoreType.DMA((9,)),
            pltpu.SemaphoreType.DMA,
            pltpu.SemaphoreType.DMA((3, 2)),
            pltpu.SemaphoreType.DMA((3, 2)),
            pltpu.SemaphoreType.DMA((CHUNKS, 2)),
            pltpu.SemaphoreType.DMA((CHUNKS, 2)),
            pltpu.SemaphoreType.DMA((CHUNKS, 4)),
            pltpu.SemaphoreType.DMA((CHUNKS, 4)),
            pltpu.SemaphoreType.DMA((CHUNKS, 3)),
            pltpu.SemaphoreType.DMA((CHUNKS, 3)),
        ],
        compiler_params=pltpu.CompilerParams(collective_id=0, has_side_effects=True, vmem_limit_bytes=32 << 20),
        name="image",
    )(*operands)


def shards(depth_cell, column_cell, row_cell, mass, counts, diffusion, tf_center, tf_sharp, tf_opacity, tf_shade, tf_color):
    forth, back, back_low, cosine = (jnp.asarray(table) for table in tables())
    cells = [cell.reshape(128, 128) for cell in (depth_cell, column_cell, row_cell)]
    extended = deposit(counts, *(pltpu.with_memory_space_constraint(x, pltpu.HBM) for x in (*cells, mass, forth)))
    return image(
        diffusion, tf_center, tf_sharp, tf_opacity, tf_shade, tf_color.T, cosine, back, back_low, extended
    )


def solution(mesh):
    brick = P("depth", "cols", None)
    placed = (brick,) * 4 + (P("depth", "cols"),) + (P(),) * 6
    return jax.shard_map(shards, mesh=mesh, in_specs=placed, out_specs=brick, check_vma=False)
```

```python
import functools

import jax
import jax.numpy as jnp
import numpy as np
from jax import lax
from jax.experimental import pallas as pl
from jax.experimental.pallas import tpu as pltpu
from jax.sharding import PartitionSpec as P

CZ, CX, CY, RIM = 16, 256, 128, 4
SMOOTH, TFS = 4, 8
HALO = SMOOTH + 1
DEEP = CZ + 2 * HALO
PLANE = 288
XO = 16
ROWS = CZ * PLANE
WIN = 112
UNROLL = 32
SLOTS = 16384
NBLK = SLOTS // 256
MESH = pl.DeviceIdType.MESH
F32, BF16 = jnp.float32, jnp.bfloat16


def split(matrix):
    top = matrix.astype(BF16)
    return top, (matrix - top.astype(np.float64)).astype(BF16)


def tables():
    n = np.arange(1, CY + 1, dtype=np.float64)
    sine = np.sqrt(2.0 / (CY + 1)) * np.sin(np.pi * np.outer(n, n) / (CY + 1))
    slope = 0.5 * (np.eye(CY, k=-1) - np.eye(CY, k=1))
    s_top, s_low = split(sine)
    b_top, b_low = split(np.concatenate([sine, sine @ slope], axis=1))
    cosine = np.broadcast_to(2.0 * np.cos(np.pi * n / (CY + 1)), (8, CY)).astype(np.float32)
    forth = np.block([[s_top, s_low], [s_top, np.zeros_like(s_low)]])
    return forth, np.concatenate([b_top, b_top]), b_low, cosine


def pair_of(value):
    top = value.astype(BF16)
    return top, (value - top.astype(F32)).astype(BF16)


def exchange(x, stride, axis, bit):
    size = x.shape[axis]
    up = pltpu.roll(x, size - stride, axis)
    down = up if 2 * stride == size else pltpu.roll(x, stride, axis)
    return jnp.where(bit, jnp.maximum(x, down), jnp.minimum(x, up))


def bitonic(vs):
    lane = lax.broadcasted_iota(jnp.int32, (8, 128), 1)
    sub = lax.broadcasted_iota(jnp.int32, (8, 128), 0)
    bits = {j: (sub >> (j - 4)) & 1 if j < 7 else (lane >> (j - 7)) & 1 for j in range(4, 14)}
    hot = {j: bits[j] == 1 for j in bits}
    neg = {j: -bits[j] for j in bits}

    def flips(j, i):
        if j == 0 or j == 14:
            return 0
        return -((i >> j) & 1) if j < 4 else neg[j]

    for k in range(1, 15):
        out = []
        for i, v in enumerate(vs):
            a, b = flips(k - 1, i), flips(k, i)
            if isinstance(a, int) and isinstance(b, int):
                out.append(~v if a != b else v)
            else:
                out.append(v ^ (a ^ b))
        vs = out
        for j in range(k - 1, 6 if k == 14 else -1, -1):
            if j >= 7:
                vs = [exchange(v, 1 << (j - 7), 1, hot[j]) for v in vs]
            elif j >= 4:
                vs = [exchange(v, 1 << (j - 4), 0, hot[j]) for v in vs]
            else:
                out = list(vs)
                for i in range(16):
                    p = i ^ (1 << j)
                    if i < p:
                        out[i] = jnp.minimum(vs[i], vs[p])
                        out[p] = jnp.maximum(vs[i], vs[p])
                vs = out
    return vs


def deposit_kernel(count, zh, xh, yh, mh, fh, out, acc, zc, xc, yc, mass, forth, wide, raw, tidy, range_of, ends, sem):
    loads = [
        pltpu.make_async_copy(source, target, sem.at[n])
        for n, (source, target) in enumerate(((mh, mass), (zh, zc), (xh, xc), (yh, yc), (fh, forth)))
    ]
    for load in loads:
        load.start()
    zeros = jnp.zeros((PLANE, 128), F32)

    @pl.loop(0, CZ)
    def _(z):
        acc[pl.ds(pl.multiple_of(z * PLANE, 8), PLANE), :] = zeros

    loads[0].wait()
    for i in range(128):
        wide[i : i + 1, :] = mass[0, 0:1, 128 * i : 128 * i + 128].astype(F32)
    for load in loads[1:]:
        load.wait()
    slot = 128 * lax.broadcasted_iota(jnp.int32, (8, 128), 0) + lax.broadcasted_iota(jnp.int32, (8, 128), 1)
    live = count[0, 0]
    keys = []
    for i in range(16):
        at = pl.ds(8 * i, 8)
        weight = jnp.where(slot + 1024 * i < live, wide[at, :] * 64.0, 0.0).astype(jnp.int32)
        row = zc[at, :] * PLANE + xc[at, :] + (XO - RIM - 4096)
        keys.append((row << 19) | (yc[at, :] << 12) | weight)
    keys = bitonic(keys)
    range_of[0] = jnp.broadcast_to(jnp.min(functools.reduce(jnp.minimum, keys), axis=0, keepdims=True), (8, 128))
    range_of[1] = jnp.broadcast_to(jnp.max(functools.reduce(jnp.maximum, keys), axis=0, keepdims=True), (8, 128))
    found = pltpu.make_async_copy(range_of, ends, sem.at[5])
    found.start()
    for i in range(16):
        raw[8 * i : 8 * i + 8, :] = keys[i]
    tidy[...] = raw[...].T
    found.wait()
    ys = lax.broadcasted_iota(jnp.int32, (128, 128), 0).astype(F32).astype(BF16)
    ws = lax.broadcasted_iota(jnp.int32, (WIN, 128), 0).astype(F32).astype(BF16)
    one, none = jnp.ones((), BF16), jnp.zeros((), BF16)

    def block(b, start, begin):
        hots, y_hots = [], []
        for half in range(2):
            key = tidy[pl.ds(2 * b + half, 1), :]
            row = (key >> 19) + 4096
            if begin is not None:
                row = jnp.where(row >= begin, row, -1)
            hots.append(jnp.where(ws == (row - start).astype(F32).astype(BF16), one, none))
            weight = ((key & 4095).astype(F32) * (1.0 / 64.0)).astype(BF16)
            y_hots.append(jnp.where(ys == ((key >> 12) & 127).astype(F32).astype(BF16), weight, none))
        hot, y_hot = jnp.concatenate(hots, axis=1), jnp.concatenate(y_hots, axis=1)
        return lax.dot_general(hot, y_hot, (((1,), (1,)), ((), ())), preferred_element_type=F32)

    def bounds(b):
        lo = (ends[0, 0, 2 * b] >> 19) + 4096
        hi = (ends[1, 0, 2 * b + 1] >> 19) + 4096
        start = jnp.minimum((lo >> 3) << 3, ROWS - WIN)
        return pl.multiple_of(start, 8), (hi - start) // WIN

    @pl.loop(0, NBLK // UNROLL)
    def _(g):
        extra = 0
        parts = []
        for u in range(UNROLL):
            b = g * UNROLL + u
            start, more = bounds(b)
            parts.append((start, block(b, start, None)))
            extra = extra + more
        for start, part in parts:
            acc[pl.ds(start, WIN), :] += part

        @pl.when(extra > 0)
        def _():
            @pl.loop(0, UNROLL)
            def _(u):
                b = g * UNROLL + u
                start, more = bounds(b)

                @pl.loop(0, more)
                def _(n):
                    begin = start + (n + 1) * WIN
                    place = pl.multiple_of(jnp.minimum(begin, ROWS - WIN), 8)
                    acc[pl.ds(place, WIN), :] += block(b, place, begin)

    both = jnp.dot(jnp.concatenate(pair_of(acc[...]), axis=1), forth[...], preferred_element_type=F32)
    out[...] = (both[:, :CY] + both[:, CY:]).reshape(CZ, PLANE, CY)


def deposit(count, zc, xc, yc, mass, forth):
    hbm = pl.BlockSpec(memory_space=pltpu.HBM)
    return pl.pallas_call(
        deposit_kernel,
        out_shape=jax.ShapeDtypeStruct((CZ, PLANE, CY), F32),
        in_specs=[pl.BlockSpec(memory_space=pltpu.SMEM)] + [hbm] * 5,
        out_specs=pl.BlockSpec(memory_space=pltpu.VMEM),
        scratch_shapes=[
            pltpu.VMEM((ROWS, CY), F32),
            pltpu.VMEM((128, 128), jnp.int32),
            pltpu.VMEM((128, 128), jnp.int32),
            pltpu.VMEM((128, 128), jnp.int32),
            pltpu.VMEM((1, 1, SLOTS), BF16),
            pltpu.VMEM((2 * CY, 2 * CY), BF16),
            pltpu.VMEM((128, 128), F32),
            pltpu.VMEM((128, 128), jnp.int32),
            pltpu.VMEM((128, 128), jnp.int32),
            pltpu.VMEM((2, 8, 128), jnp.int32),
            pltpu.SMEM((2, 8, 128), jnp.int32),
            pltpu.SemaphoreType.DMA((6,)),
        ],
        compiler_params=pltpu.CompilerParams(vmem_limit_bytes=12 << 20),
        name="deposit",
    )(count, zc, xc, yc, mass, forth)


CHUNK = 64
CHUNKS = CX // CHUNK
SPAN = CHUNK + 16
ORDER = (1, 2, 0, 3)
PARTS = ((64, 96), (160, 64), (8, 56), (224, 56))


def sweep(src, at, dst, lo, hi, unroll, center, ratio, x_live):
    @pl.loop(0, (hi - lo) // unroll)
    def _(step):
        for n in range(SPAN // 8):
            r = at + 8 * n
            for u in range(unroll):
                z = lo + step * unroll + u
                along_z = src[z - 1, r : r + 8, :] + src[z + 1, r : r + 8, :]
                along_x = src[z, r - 1 : r + 7, :] + src[z, r + 1 : r + 9, :]
                new = src[z, r : r + 8, :] * center + along_x * ratio + along_z
                if n in x_live:
                    new = new * x_live[n]
                dst[z, 8 + 8 * n : 16 + 8 * n, :] = new


def back_to_cells(src, dst, grad, back, back_low, scale):
    rows = 6 * SPAN

    @pl.loop(0, (CZ + 2) // 6)
    def _(step):
        z = step * 6
        top, rest = pair_of(src[pl.ds(z + HALO - 1, 6), 8 : 8 + SPAN, :].reshape(rows, CY) * scale)
        mixed = jnp.dot(jnp.concatenate([top, rest], axis=1), back[...], preferred_element_type=F32)
        mixed = (mixed + jnp.dot(top, back_low[...], preferred_element_type=F32)).reshape(6, SPAN, 2 * CY)
        dst[pl.ds(z + HALO - 1, 6), 8 : 8 + SPAN, :] = mixed[:, :, :CY]
        grad[pl.ds(z, 6)] = mixed[:, 8 : 8 + CHUNK, CY:]


def gradient(src, grad, rise_d, rise_g):
    for n in range(CHUNK // 8):
        r, at = 16 + 8 * n, slice(8 * n, 8 * n + 8)
        for z in range(CZ):
            here = src[z + HALO, r : r + 8, :]
            before = src[z + HALO - 1, r : r + 8, :]
            gz = src[z + HALO + 1, r : r + 8, :] - before
            gx = src[z + HALO, r + 1 : r + 9, :] - src[z + HALO, r - 1 : r + 7, :]
            gy = grad[z + 1, at, :]
            square = (gz * gz + gx * gx) * 0.25 + gy * gy
            if z == 0:
                rise_g[0, at, :] = square
            else:
                rise_g[z, at, :] = square - last
                rise_d[z, at, :] = here - before
            last = square
        rise_g[CZ, at, :] = last


def render(dens, rise_d, rise_g, out, slope, shift, scale):
    rows = slice(16, 16 + CHUNK)
    over = 1.0 - scale
    sum_d, sum_g = dens[HALO, rows, :], rise_g[0]
    for z in range(CZ):
        t = jnp.tanh(dens[z + HALO, rows, :] * slope + shift)
        through = over - t * scale
        if z == 0:
            keep = through
        else:
            sum_d = sum_d + keep * rise_d[z]
            sum_g = sum_g + keep * rise_g[z]
            keep = keep * through
    out[0] = sum_d - keep * dens[HALO + CZ - 1, rows, :]
    out[1] = sum_g - keep * rise_g[CZ]
    out[2] = keep


def image_kernel(
    dif_h, tfc_h, tfs_h, tfo_h, shade_h, tint_h, cosine_h, back_h, low_h, ext, out,
    one, ta, tb, left, right, grad, rise_d, rise_g, mine, came, whole,
    dif, tfc, tfs, tfo, shade, tint, cosine, back, back_low,
    load_sem, local_sem, side_send, side_recv, halo_send, halo_recv, pair_send, pair_recv, far_send, far_recv,
):
    depth, cols = lax.axis_index("depth"), lax.axis_index("cols")
    nd, nc = lax.axis_size("depth"), lax.axis_size("cols")
    core, chip = depth % 2, depth // 2
    chips = nd // 2
    partner = (depth + 1 - 2 * core, cols)

    exists = {(-1, 0): depth > 0, (1, 0): depth < nd - 1, (0, -1): cols > 0, (0, 1): cols < nc - 1}
    barrier = pltpu.get_barrier_semaphore()

    def greet(device):
        pl.semaphore_signal(barrier, inc=1, device_id=device, device_id_type=MESH)

    for dz, dx in exists:
        pl.when(exists[dz, dx])(functools.partial(greet, (depth + dz, cols + dx)))
    for n in range(1, chips):
        greet(((depth + 2 * n) % nd, cols))
    pairs = (
        (dif_h, dif), (tfc_h, tfc), (tfs_h, tfs), (tfo_h, tfo), (shade_h, shade), (tint_h, tint),
        (cosine_h, cosine), (back_h, back), (low_h, back_low),
    )
    loads = [pltpu.make_async_copy(source, target, load_sem.at[n]) for n, (source, target) in enumerate(pairs)]
    inner = pltpu.make_async_copy(ext, one.at[pl.ds(HALO, CZ)], local_sem)
    inner.start()
    for load in loads:
        load.start()
    zeros = jnp.zeros((8, CY), F32)

    @pl.loop(0, DEEP)
    def _(z):
        for t in (ta, tb):
            t[z, 0:8, :] = zeros
            t[z, 8 + SPAN : 16 + SPAN, :] = zeros

    for z in (*range(HALO), *range(HALO + CZ, DEEP)):
        one[z, 0:8, :] = zeros
        one[z, 280:288, :] = zeros

    def clear(ref, first, begin, rows):
        @pl.when(depth == 0)
        def _():
            for z in range(first, HALO):
                ref[z, begin : begin + rows, :] = jnp.zeros((rows, CY), F32)

        @pl.when(depth == nd - 1)
        def _():
            for z in range(HALO + CZ, DEEP - first):
                ref[z, begin : begin + rows, :] = jnp.zeros((rows, CY), F32)

    clear(one, 0, 8, 272)

    @pl.when(cols == 0)
    def _():
        left[...] = jnp.zeros((DEEP, 16, CY), F32)

    @pl.when(cols == nc - 1)
    def _():
        right[...] = jnp.zeros((DEEP, 16, CY), F32)

    pl.semaphore_wait(barrier, sum(near.astype(jnp.int32) for near in exists.values()) + chips - 1)

    planes = {1: (CZ - HALO, 0, HALO), -1: (0, HALO + CZ, HALO)}

    def copy_of(source, target, send, recv, device):
        return pltpu.make_async_remote_copy(
            src_ref=source, dst_ref=target, send_sem=send, recv_sem=recv, device_id=device, device_id_type=MESH
        )

    def halo(step, dz, act):
        begin, rows = PARTS[step]
        src, dst, count = planes[dz]
        n = (1 + dz) // 2
        copy = copy_of(
            ext.at[pl.ds(src, count), pl.ds(begin, rows)], one.at[pl.ds(dst, count), pl.ds(begin, rows)],
            halo_send.at[step, n], halo_recv.at[step, n], (depth + dz, cols),
        )
        pl.when(exists[dz, 0])(lambda: getattr(copy, act)())

    def start_halo(step):
        for dz in (-1, 1):
            halo(step, dz, "start")

    def arrive(step):
        for dz in (-1, 1):
            halo(step, dz, "wait_send")
            begin, rows = PARTS[step]
            src, dst, count = planes[dz]
            n = (1 + dz) // 2
            copy = copy_of(
                ext.at[pl.ds(src, count), pl.ds(begin, rows)], one.at[pl.ds(dst, count), pl.ds(begin, rows)],
                halo_send.at[step, n], halo_recv.at[step, n], (depth - dz, cols),
            )
            pl.when(exists[-dz, 0])(copy.wait_recv)

    spots = ((0, CZ, HALO), (0, HALO, 0), (HALO + CZ, HALO, HALO + CZ))

    def side(n, act):
        begin, count, at = spots[n]
        source = one if n else ext
        for m, dx, target in ((0, 1, left), (1, -1, right)):
            copy = copy_of(
                source.at[pl.ds(begin, count), pl.ds(264 if dx == 1 else 8, 16)], target.at[pl.ds(at, count)],
                side_send.at[n, m], side_recv.at[n, m], (depth, cols + dx),
            )
            pl.when(exists[0, dx] if act != "wait_recv" else exists[0, -dx])(lambda: getattr(copy, act)())

    start_halo(0)
    side(0, "start")
    for later in range(1, CHUNKS):
        start_halo(later)
    inner.wait()
    for load in loads:
        load.wait()

    has_left = jnp.where(cols > 0, 1.0, 0.0)
    has_right = jnp.where(cols < nc - 1, 1.0, 0.0)
    d0, d1, d2 = dif[0], dif[1], dif[2]
    along = jnp.full((8, CY), d0, F32)
    center = (cosine[...] * d2 + (1.0 - 2.0 * (d0 + d1 + d2))) / along
    ratio = jnp.full((8, CY), d1, F32) / along
    square = d0 * d0

    def draw(chunk, own):
        @pl.loop(0, chips)
        def _(j):
            k = 2 * ((chip + j + 2) % chips) + (core if own else 1 - core)
            sharp = 0.5 * tfs[k]
            out_ref = mine.at[chunk, j + (chips if own else 0)]
            render(ta, rise_d, rise_g, out_ref, sharp, -sharp * tfc[k], 0.5 * tfo[k])
            if not own:
                swap_of(chunk, j).start()

    def swap_of(chunk, j):
        return copy_of(
            mine.at[chunk, j], came.at[chunk, j], pair_send.at[chunk, j], pair_recv.at[chunk, j], partner
        )

    sends = []

    def combine(chunk):
        for j in (0, 1, 3, 2):
            swap_of(chunk, j).wait_recv()
            i = (chip + j + 2) % chips
            held = mine.at[chunk, chips + j]
            place = whole.at[chip, chunk] if j == 2 else held
            for n in range(CHUNK // 32):
                at = pl.ds(32 * n, 32)
                first = [jnp.where(core == 0, held[q, at, :], came[chunk, j, q, at, :]) for q in range(3)]
                then = [jnp.where(core == 0, came[chunk, j, q, at, :], held[q, at, :]) for q in range(3)]
                place[0, at, :] = first[0] + first[2] * then[0]
                place[1, at, :] = first[1] + first[2] * then[1]
                place[2, at, :] = first[2] * then[2]
            if j != 2:
                m = j - j // 3
                send = copy_of(
                    held, whole.at[chip, chunk], far_send.at[chunk, m], far_recv.at[chunk, m], (2 * i + core, cols)
                )
                send.start()
                sends.append(send)

    for step in range(CHUNKS):
        chunk = ORDER[step]
        if step < CHUNKS - 2:
            arrive(step)
        if step == CHUNKS - 2:
            for n in range(3):
                side(n, "wait_send")
                side(n, "wait_recv")

            @pl.loop(0, DEEP)
            def _(z):
                one[z, 8:16, :] = (one[z, 8:16, :] + left[z, 0:8, :]) * has_left
                one[z, 16:24, :] = one[z, 16:24, :] + left[z, 8:16, :] * has_left
                one[z, 264:272, :] = one[z, 264:272, :] + right[z, 0:8, :] * has_right
                one[z, 272:280, :] = (one[z, 272:280, :] + right[z, 8:16, :]) * has_right
        x_live = {0: has_left} if chunk == 0 else {SPAN // 8 - 1: has_right} if chunk == CHUNKS - 1 else {}
        sweep(one, 8 + CHUNK * chunk, ta, 1, DEEP - 1, 8, center, ratio, x_live)
        clear(ta, 1, 8, SPAN)
        if step:
            combine(ORDER[step - 1])
        sweep(ta, 8, tb, 2, DEEP - 2, 11, center, ratio, x_live)
        clear(tb, 2, 8, SPAN)
        sweep(tb, 8, ta, 3, DEEP - 3, 10, center, ratio, x_live)
        clear(ta, 3, 8, SPAN)
        sweep(ta, 8, tb, 4, DEEP - 4, 9, center, ratio, x_live)
        clear(tb, 4, 8, SPAN)
        if step == CHUNKS // 2 - 1:
            arrive(CHUNKS - 2)
            arrive(CHUNKS - 1)
            side(1, "start")
            side(2, "start")
        back_to_cells(tb, ta, grad, back, back_low, square * square)
        gradient(ta, grad, rise_d, rise_g)
        draw(chunk, False)
        draw(chunk, True)
    combine(ORDER[-1])

    color = [tint[q, depth] for q in range(3)]
    shading = shade[depth]
    for step in range(CHUNKS):
        for send in sends[3 * step : 3 * step + 3]:
            send.wait()
        chunk = ORDER[step]
        for n in range(CHUNK // 32):
            at = pl.ds(32 * n, 32)
            to = pl.ds(CHUNK * chunk + 32 * n, 32)
            sum_d, sum_g, keep = (whole[chips - 1, chunk, q, at, :] for q in range(3))
            for i in range(chips - 2, -1, -1):
                near = whole[i, chunk, 2, at, :]
                sum_d = whole[i, chunk, 0, at, :] + near * sum_d
                sum_g = whole[i, chunk, 1, at, :] + near * sum_g
                keep = near * keep
            for q in range(3):
                out[q, to, :] = sum_d * color[q] + sum_g * shading
            out[3, to, :] = keep
    for chunk in ORDER:
        for j in range(chips):
            swap_of(chunk, j).wait_send()


def image(*operands):
    tall = pltpu.VMEM((DEEP, SPAN + 16, CY), F32)
    strip = pltpu.VMEM((DEEP, 16, CY), F32)
    return pl.pallas_call(
        image_kernel,
        out_shape=jax.ShapeDtypeStruct((4, CX, CY), F32),
        in_specs=[pl.BlockSpec(memory_space=pl.ANY)] * 10,
        out_specs=pl.BlockSpec(memory_space=pltpu.VMEM),
        scratch_shapes=[
            pltpu.VMEM((DEEP, PLANE, CY), F32),
            tall,
            tall,
            strip,
            strip,
            pltpu.VMEM((CZ + 2, CHUNK, CY), F32),
            pltpu.VMEM((CZ, CHUNK, CY), F32),
            pltpu.VMEM((CZ + 1, CHUNK, CY), F32),
            pltpu.VMEM((CHUNKS, TFS, 3, CHUNK, CY), F32),
            pltpu.VMEM((CHUNKS, 4, 3, CHUNK, CY), F32),
            pltpu.VMEM((4, CHUNKS, 3, CHUNK, CY), F32),
            pltpu.SMEM((3,), F32),
            *[pltpu.SMEM((TFS,), F32)] * 4,
            pltpu.SMEM((3, TFS), F32),
            pltpu.VMEM((8, CY), F32),
            pltpu.VMEM((2 * CY, 2 * CY), BF16),
            pltpu.VMEM((CY, 2 * CY), BF16),
            pltpu.SemaphoreType.DMA((9,)),
            pltpu.SemaphoreType.DMA,
            pltpu.SemaphoreType.DMA((3, 2)),
            pltpu.SemaphoreType.DMA((3, 2)),
            pltpu.SemaphoreType.DMA((CHUNKS, 2)),
            pltpu.SemaphoreType.DMA((CHUNKS, 2)),
            pltpu.SemaphoreType.DMA((CHUNKS, 4)),
            pltpu.SemaphoreType.DMA((CHUNKS, 4)),
            pltpu.SemaphoreType.DMA((CHUNKS, 3)),
            pltpu.SemaphoreType.DMA((CHUNKS, 3)),
        ],
        compiler_params=pltpu.CompilerParams(collective_id=0, has_side_effects=True, vmem_limit_bytes=32 << 20),
        name="image",
    )(*operands)


def shards(depth_cell, column_cell, row_cell, mass, counts, diffusion, tf_center, tf_sharp, tf_opacity, tf_shade, tf_color):
    forth, back, back_low, cosine = (jnp.asarray(table) for table in tables())
    cells = [cell.reshape(128, 128) for cell in (depth_cell, column_cell, row_cell)]
    extended = deposit(counts, *(pltpu.with_memory_space_constraint(x, pltpu.HBM) for x in (*cells, mass, forth)))
    return image(
        diffusion, tf_center, tf_sharp, tf_opacity, tf_shade, tf_color.T, cosine, back, back_low, extended
    )


def solution(mesh):
    brick = P("depth", "cols", None)
    placed = (brick,) * 4 + (P("depth", "cols"),) + (P(),) * 6
    return jax.shard_map(shards, mesh=mesh, in_specs=placed, out_specs=brick, check_vma=False)
```

```python
import functools

import jax
import jax.numpy as jnp
import numpy as np
from jax import lax
from jax.experimental import pallas as pl
from jax.experimental.pallas import tpu as pltpu
from jax.sharding import PartitionSpec as P

CZ, CX, CY, RIM = 16, 256, 128, 4
SMOOTH, TFS = 4, 8
HALO = SMOOTH + 1
DEEP = CZ + 2 * HALO
PLANE = 288
XO = 16
ROWS = CZ * PLANE
WIN = 112
UNROLL = 32
SLOTS = 16384
NBLK = SLOTS // 256
MESH = pl.DeviceIdType.MESH
F32, BF16 = jnp.float32, jnp.bfloat16


def split(matrix):
    top = matrix.astype(BF16)
    return top, (matrix - top.astype(np.float64)).astype(BF16)


def tables():
    n = np.arange(1, CY + 1, dtype=np.float64)
    sine = np.sqrt(2.0 / (CY + 1)) * np.sin(np.pi * np.outer(n, n) / (CY + 1))
    slope = 0.5 * (np.eye(CY, k=-1) - np.eye(CY, k=1))
    s_top, s_low = split(sine)
    b_top, b_low = split(np.concatenate([sine, sine @ slope], axis=1))
    cosine = np.broadcast_to(2.0 * np.cos(np.pi * n / (CY + 1)), (8, CY)).astype(np.float32)
    forth = np.block([[s_top, s_low], [s_top, np.zeros_like(s_low)]])
    return forth, np.concatenate([b_top, b_top]), b_low, cosine


def pair_of(value):
    top = value.astype(BF16)
    return top, (value - top.astype(F32)).astype(BF16)


def exchange(x, stride, axis, bit):
    size = x.shape[axis]
    up = pltpu.roll(x, size - stride, axis)
    down = up if 2 * stride == size else pltpu.roll(x, stride, axis)
    return jnp.where(bit, jnp.maximum(x, down), jnp.minimum(x, up))


def bitonic(vs):
    lane = lax.broadcasted_iota(jnp.int32, (8, 128), 1)
    sub = lax.broadcasted_iota(jnp.int32, (8, 128), 0)
    bits = {j: (sub >> (j - 4)) & 1 if j < 7 else (lane >> (j - 7)) & 1 for j in range(4, 14)}
    hot = {j: bits[j] == 1 for j in bits}
    neg = {j: -bits[j] for j in bits}

    def flips(j, i):
        if j == 0 or j == 14:
            return 0
        return -((i >> j) & 1) if j < 4 else neg[j]

    for k in range(1, 15):
        out = []
        for i, v in enumerate(vs):
            a, b = flips(k - 1, i), flips(k, i)
            if isinstance(a, int) and isinstance(b, int):
                out.append(~v if a != b else v)
            else:
                out.append(v ^ (a ^ b))
        vs = out
        for j in range(k - 1, 6 if k == 14 else -1, -1):
            if j >= 7:
                vs = [exchange(v, 1 << (j - 7), 1, hot[j]) for v in vs]
            elif j >= 4:
                vs = [exchange(v, 1 << (j - 4), 0, hot[j]) for v in vs]
            else:
                out = list(vs)
                for i in range(16):
                    p = i ^ (1 << j)
                    if i < p:
                        out[i] = jnp.minimum(vs[i], vs[p])
                        out[p] = jnp.maximum(vs[i], vs[p])
                vs = out
    return vs


def deposit_kernel(count, zh, xh, yh, mh, fh, out, acc, zc, xc, yc, mass, forth, wide, raw, tidy, range_of, ends, sem):
    loads = [
        pltpu.make_async_copy(source, target, sem.at[n])
        for n, (source, target) in enumerate(((mh, mass), (zh, zc), (xh, xc), (yh, yc), (fh, forth)))
    ]
    for load in loads:
        load.start()
    zeros = jnp.zeros((PLANE, 128), F32)

    @pl.loop(0, CZ)
    def _(z):
        acc[pl.ds(pl.multiple_of(z * PLANE, 8), PLANE), :] = zeros

    loads[0].wait()
    for i in range(128):
        wide[i : i + 1, :] = mass[0, 0:1, 128 * i : 128 * i + 128].astype(F32)
    for load in loads[1:]:
        load.wait()
    slot = 128 * lax.broadcasted_iota(jnp.int32, (8, 128), 0) + lax.broadcasted_iota(jnp.int32, (8, 128), 1)
    live = count[0, 0]
    keys = []
    for i in range(16):
        at = pl.ds(8 * i, 8)
        weight = jnp.where(slot + 1024 * i < live, wide[at, :] * 64.0, 0.0).astype(jnp.int32)
        row = zc[at, :] * PLANE + xc[at, :] + (XO - RIM - 4096)
        keys.append((row << 19) | (yc[at, :] << 12) | weight)
    keys = bitonic(keys)
    range_of[0] = jnp.broadcast_to(jnp.min(functools.reduce(jnp.minimum, keys), axis=0, keepdims=True), (8, 128))
    range_of[1] = jnp.broadcast_to(jnp.max(functools.reduce(jnp.maximum, keys), axis=0, keepdims=True), (8, 128))
    found = pltpu.make_async_copy(range_of, ends, sem.at[5])
    found.start()
    for i in range(16):
        raw[8 * i : 8 * i + 8, :] = keys[i]
    tidy[...] = raw[...].T
    found.wait()
    ys = lax.broadcasted_iota(jnp.int32, (128, 128), 0).astype(F32).astype(BF16)
    ws = lax.broadcasted_iota(jnp.int32, (WIN, 128), 0).astype(F32).astype(BF16)
    one, none = jnp.ones((), BF16), jnp.zeros((), BF16)

    def block(b, start, begin):
        hots, y_hots = [], []
        for half in range(2):
            key = tidy[pl.ds(2 * b + half, 1), :]
            row = (key >> 19) + 4096
            if begin is not None:
                row = jnp.where(row >= begin, row, -1)
            hots.append(jnp.where(ws == (row - start).astype(F32).astype(BF16), one, none))
            weight = ((key & 4095).astype(F32) * (1.0 / 64.0)).astype(BF16)
            y_hots.append(jnp.where(ys == ((key >> 12) & 127).astype(F32).astype(BF16), weight, none))
        hot, y_hot = jnp.concatenate(hots, axis=1), jnp.concatenate(y_hots, axis=1)
        return lax.dot_general(hot, y_hot, (((1,), (1,)), ((), ())), preferred_element_type=F32)

    def bounds(b):
        lo = (ends[0, 0, 2 * b] >> 19) + 4096
        hi = (ends[1, 0, 2 * b + 1] >> 19) + 4096
        start = jnp.minimum((lo >> 3) << 3, ROWS - WIN)
        return pl.multiple_of(start, 8), (hi - start) // WIN

    @pl.loop(0, NBLK // UNROLL)
    def _(g):
        extra = 0
        parts = []
        for u in range(UNROLL):
            b = g * UNROLL + u
            start, more = bounds(b)
            parts.append((start, block(b, start, None)))
            extra = extra + more
        for start, part in parts:
            acc[pl.ds(start, WIN), :] += part

        @pl.when(extra > 0)
        def _():
            @pl.loop(0, UNROLL)
            def _(u):
                b = g * UNROLL + u
                start, more = bounds(b)

                @pl.loop(0, more)
                def _(n):
                    begin = start + (n + 1) * WIN
                    place = pl.multiple_of(jnp.minimum(begin, ROWS - WIN), 8)
                    acc[pl.ds(place, WIN), :] += block(b, place, begin)

    both = jnp.dot(jnp.concatenate(pair_of(acc[...]), axis=1), forth[...], preferred_element_type=F32)
    out[...] = (both[:, :CY] + both[:, CY:]).reshape(CZ, PLANE, CY)


def deposit(count, zc, xc, yc, mass, forth):
    hbm = pl.BlockSpec(memory_space=pltpu.HBM)
    return pl.pallas_call(
        deposit_kernel,
        out_shape=jax.ShapeDtypeStruct((CZ, PLANE, CY), F32),
        in_specs=[pl.BlockSpec(memory_space=pltpu.SMEM)] + [hbm] * 5,
        out_specs=pl.BlockSpec(memory_space=pltpu.VMEM),
        scratch_shapes=[
            pltpu.VMEM((ROWS, CY), F32),
            pltpu.VMEM((128, 128), jnp.int32),
            pltpu.VMEM((128, 128), jnp.int32),
            pltpu.VMEM((128, 128), jnp.int32),
            pltpu.VMEM((1, 1, SLOTS), BF16),
            pltpu.VMEM((2 * CY, 2 * CY), BF16),
            pltpu.VMEM((128, 128), F32),
            pltpu.VMEM((128, 128), jnp.int32),
            pltpu.VMEM((128, 128), jnp.int32),
            pltpu.VMEM((2, 8, 128), jnp.int32),
            pltpu.SMEM((2, 8, 128), jnp.int32),
            pltpu.SemaphoreType.DMA((6,)),
        ],
        compiler_params=pltpu.CompilerParams(vmem_limit_bytes=12 << 20),
        name="deposit",
    )(count, zc, xc, yc, mass, forth)


CHUNK = 64
CHUNKS = CX // CHUNK
SPAN = CHUNK + 16
ORDER = (1, 2, 0, 3)
PARTS = ((64, 96), (160, 64), (8, 56), (224, 56))


def sweep(src, at, dst, lo, hi, unroll, center, ratio, x_live):
    @pl.loop(0, (hi - lo) // unroll)
    def _(step):
        for n in range(SPAN // 8):
            r = at + 8 * n
            for u in range(unroll):
                z = lo + step * unroll + u
                along_z = src[z - 1, r : r + 8, :] + src[z + 1, r : r + 8, :]
                along_x = src[z, r - 1 : r + 7, :] + src[z, r + 1 : r + 9, :]
                new = src[z, r : r + 8, :] * center + along_x * ratio + along_z
                if n in x_live:
                    new = new * x_live[n]
                dst[z, 8 + 8 * n : 16 + 8 * n, :] = new


def back_to_cells(src, dst, grad, back, back_low, scale):
    rows = 6 * SPAN

    @pl.loop(0, (CZ + 2) // 6)
    def _(step):
        z = step * 6
        top, rest = pair_of(src[pl.ds(z + HALO - 1, 6), 8 : 8 + SPAN, :].reshape(rows, CY) * scale)
        mixed = jnp.dot(jnp.concatenate([top, rest], axis=1), back[...], preferred_element_type=F32)
        mixed = (mixed + jnp.dot(top, back_low[...], preferred_element_type=F32)).reshape(6, SPAN, 2 * CY)
        dst[pl.ds(z + HALO - 1, 6), 8 : 8 + SPAN, :] = mixed[:, :, :CY]
        grad[pl.ds(z, 6)] = mixed[:, 8 : 8 + CHUNK, CY:]


def gradient(src, grad, rise_d, rise_g):
    for n in range(CHUNK // 8):
        r, at = 16 + 8 * n, slice(8 * n, 8 * n + 8)
        for z in range(CZ):
            here = src[z + HALO, r : r + 8, :]
            before = src[z + HALO - 1, r : r + 8, :]
            gz = src[z + HALO + 1, r : r + 8, :] - before
            gx = src[z + HALO, r + 1 : r + 9, :] - src[z + HALO, r - 1 : r + 7, :]
            gy = grad[z + 1, at, :]
            square = (gz * gz + gx * gx) * 0.25 + gy * gy
            if z == 0:
                rise_g[0, at, :] = square
            else:
                rise_g[z, at, :] = square - last
                rise_d[z, at, :] = here - before
            last = square
        rise_g[CZ, at, :] = last


def render(dens, rise_d, rise_g, out, slope, shift, scale):
    rows = slice(16, 16 + CHUNK)
    over = 1.0 - scale
    sum_d, sum_g = dens[HALO, rows, :], rise_g[0]
    for z in range(CZ):
        t = jnp.tanh(dens[z + HALO, rows, :] * slope + shift)
        through = over - t * scale
        if z == 0:
            keep = through
        else:
            sum_d = sum_d + keep * rise_d[z]
            sum_g = sum_g + keep * rise_g[z]
            keep = keep * through
    out[0] = sum_d - keep * dens[HALO + CZ - 1, rows, :]
    out[1] = sum_g - keep * rise_g[CZ]
    out[2] = keep


def image_kernel(
    dif_h, tfc_h, tfs_h, tfo_h, shade_h, tint_h, cosine_h, back_h, low_h, ext, out,
    one, ta, tb, left, right, grad, rise_d, rise_g, mine, came, whole,
    dif, tfc, tfs, tfo, shade, tint, cosine, back, back_low,
    load_sem, local_sem, side_send, side_recv, halo_send, halo_recv, pair_send, pair_recv, far_send, far_recv,
):
    depth, cols = lax.axis_index("depth"), lax.axis_index("cols")
    nd, nc = lax.axis_size("depth"), lax.axis_size("cols")
    core, chip = depth % 2, depth // 2
    chips = nd // 2
    partner = (depth + 1 - 2 * core, cols)

    exists = {(-1, 0): depth > 0, (1, 0): depth < nd - 1, (0, -1): cols > 0, (0, 1): cols < nc - 1}
    barrier = pltpu.get_barrier_semaphore()

    def greet(device):
        pl.semaphore_signal(barrier, inc=1, device_id=device, device_id_type=MESH)

    for dz, dx in exists:
        pl.when(exists[dz, dx])(functools.partial(greet, (depth + dz, cols + dx)))
    for n in range(1, chips):
        greet(((depth + 2 * n) % nd, cols))
    pairs = (
        (dif_h, dif), (tfc_h, tfc), (tfs_h, tfs), (tfo_h, tfo), (shade_h, shade), (tint_h, tint),
        (cosine_h, cosine), (back_h, back), (low_h, back_low),
    )
    loads = [pltpu.make_async_copy(source, target, load_sem.at[n]) for n, (source, target) in enumerate(pairs)]
    inner = pltpu.make_async_copy(ext, one.at[pl.ds(HALO, CZ)], local_sem)
    inner.start()
    for load in loads:
        load.start()
    zeros = jnp.zeros((8, CY), F32)

    @pl.loop(0, DEEP)
    def _(z):
        for t in (ta, tb):
            t[z, 0:8, :] = zeros
            t[z, 8 + SPAN : 16 + SPAN, :] = zeros

    for z in (*range(HALO), *range(HALO + CZ, DEEP)):
        one[z, 0:8, :] = zeros
        one[z, 280:288, :] = zeros

    def clear(ref, first, begin, rows):
        @pl.when(depth == 0)
        def _():
            for z in range(first, HALO):
                ref[z, begin : begin + rows, :] = jnp.zeros((rows, CY), F32)

        @pl.when(depth == nd - 1)
        def _():
            for z in range(HALO + CZ, DEEP - first):
                ref[z, begin : begin + rows, :] = jnp.zeros((rows, CY), F32)

    clear(one, 0, 8, 272)

    @pl.when(cols == 0)
    def _():
        left[...] = jnp.zeros((DEEP, 16, CY), F32)

    @pl.when(cols == nc - 1)
    def _():
        right[...] = jnp.zeros((DEEP, 16, CY), F32)

    pl.semaphore_wait(barrier, sum(near.astype(jnp.int32) for near in exists.values()) + chips - 1)

    planes = {1: (CZ - HALO, 0, HALO), -1: (0, HALO + CZ, HALO)}

    def copy_of(source, target, send, recv, device):
        return pltpu.make_async_remote_copy(
            src_ref=source, dst_ref=target, send_sem=send, recv_sem=recv, device_id=device, device_id_type=MESH
        )

    def halo(step, dz, act):
        begin, rows = PARTS[step]
        src, dst, count = planes[dz]
        n = (1 + dz) // 2
        copy = copy_of(
            ext.at[pl.ds(src, count), pl.ds(begin, rows)], one.at[pl.ds(dst, count), pl.ds(begin, rows)],
            halo_send.at[step, n], halo_recv.at[step, n], (depth + dz, cols),
        )
        pl.when(exists[dz, 0])(lambda: getattr(copy, act)())

    def start_halo(step):
        for dz in (-1, 1):
            halo(step, dz, "start")

    def arrive(step):
        for dz in (-1, 1):
            halo(step, dz, "wait_send")
            begin, rows = PARTS[step]
            src, dst, count = planes[dz]
            n = (1 + dz) // 2
            copy = copy_of(
                ext.at[pl.ds(src, count), pl.ds(begin, rows)], one.at[pl.ds(dst, count), pl.ds(begin, rows)],
                halo_send.at[step, n], halo_recv.at[step, n], (depth - dz, cols),
            )
            pl.when(exists[-dz, 0])(copy.wait_recv)

    spots = ((0, CZ, HALO), (0, HALO, 0), (HALO + CZ, HALO, HALO + CZ))

    def side(n, act):
        begin, count, at = spots[n]
        source = one if n else ext
        for m, dx, target in ((0, 1, left), (1, -1, right)):
            copy = copy_of(
                source.at[pl.ds(begin, count), pl.ds(264 if dx == 1 else 8, 16)], target.at[pl.ds(at, count)],
                side_send.at[n, m], side_recv.at[n, m], (depth, cols + dx),
            )
            pl.when(exists[0, dx] if act != "wait_recv" else exists[0, -dx])(lambda: getattr(copy, act)())

    start_halo(0)
    side(0, "start")
    for later in range(1, CHUNKS):
        start_halo(later)
    inner.wait()
    for load in loads:
        load.wait()

    has_left = jnp.where(cols > 0, 1.0, 0.0)
    has_right = jnp.where(cols < nc - 1, 1.0, 0.0)
    d0, d1, d2 = dif[0], dif[1], dif[2]
    along = jnp.full((8, CY), d0, F32)
    center = (cosine[...] * d2 + (1.0 - 2.0 * (d0 + d1 + d2))) / along
    ratio = jnp.full((8, CY), d1, F32) / along
    square = d0 * d0

    def draw(chunk, own):
        @pl.loop(0, chips)
        def _(j):
            owner = core if own else 1 - core
            k = 2 * ((chip + jnp.where(owner == 0, j + 2, 6 - j)) % chips) + owner
            sharp = 0.5 * tfs[k]
            out_ref = mine.at[chunk, j + (chips if own else 0)]
            render(ta, rise_d, rise_g, out_ref, sharp, -sharp * tfc[k], 0.5 * tfo[k])
            if not own:
                swap_of(chunk, j).start()

    def swap_of(chunk, j):
        return copy_of(
            mine.at[chunk, j], came.at[chunk, j], pair_send.at[chunk, j], pair_recv.at[chunk, j], partner
        )

    sends = []

    def combine(chunk):
        for j in (0, 1, 3, 2):
            swap_of(chunk, j).wait_recv()
            i = (chip + jnp.where(core == 0, j + 2, 6 - j)) % chips
            held = mine.at[chunk, chips + j]
            place = whole.at[chip, chunk] if j == 2 else held
            for n in range(CHUNK // 32):
                at = pl.ds(32 * n, 32)
                first = [jnp.where(core == 0, held[q, at, :], came[chunk, j, q, at, :]) for q in range(3)]
                then = [jnp.where(core == 0, came[chunk, j, q, at, :], held[q, at, :]) for q in range(3)]
                place[0, at, :] = first[0] + first[2] * then[0]
                place[1, at, :] = first[1] + first[2] * then[1]
                place[2, at, :] = first[2] * then[2]
            if j != 2:
                m = j - j // 3
                send = copy_of(
                    held, whole.at[chip, chunk], far_send.at[chunk, m], far_recv.at[chunk, m], (2 * i + core, cols)
                )
                send.start()
                sends.append(send)

    for step in range(CHUNKS):
        chunk = ORDER[step]
        if step < CHUNKS - 2:
            arrive(step)
        if step == CHUNKS - 2:
            for n in range(3):
                side(n, "wait_send")
                side(n, "wait_recv")

            @pl.loop(0, DEEP)
            def _(z):
                one[z, 8:16, :] = (one[z, 8:16, :] + left[z, 0:8, :]) * has_left
                one[z, 16:24, :] = one[z, 16:24, :] + left[z, 8:16, :] * has_left
                one[z, 264:272, :] = one[z, 264:272, :] + right[z, 0:8, :] * has_right
                one[z, 272:280, :] = (one[z, 272:280, :] + right[z, 8:16, :]) * has_right
        x_live = {0: has_left} if chunk == 0 else {SPAN // 8 - 1: has_right} if chunk == CHUNKS - 1 else {}
        sweep(one, 8 + CHUNK * chunk, ta, 1, DEEP - 1, 8, center, ratio, x_live)
        clear(ta, 1, 8, SPAN)
        if step:
            combine(ORDER[step - 1])
        sweep(ta, 8, tb, 2, DEEP - 2, 11, center, ratio, x_live)
        clear(tb, 2, 8, SPAN)
        sweep(tb, 8, ta, 3, DEEP - 3, 10, center, ratio, x_live)
        clear(ta, 3, 8, SPAN)
        sweep(ta, 8, tb, 4, DEEP - 4, 9, center, ratio, x_live)
        clear(tb, 4, 8, SPAN)
        if step == CHUNKS // 2 - 1:
            arrive(CHUNKS - 2)
            arrive(CHUNKS - 1)
            side(1, "start")
            side(2, "start")
        back_to_cells(tb, ta, grad, back, back_low, square * square)
        gradient(ta, grad, rise_d, rise_g)
        draw(chunk, False)
        draw(chunk, True)
    combine(ORDER[-1])

    color = [tint[q, depth] for q in range(3)]
    shading = shade[depth]
    for step in range(CHUNKS):
        for send in sends[3 * step : 3 * step + 3]:
            send.wait()
        chunk = ORDER[step]
        for n in range(CHUNK // 32):
            at = pl.ds(32 * n, 32)
            to = pl.ds(CHUNK * chunk + 32 * n, 32)
            sum_d, sum_g, keep = (whole[chips - 1, chunk, q, at, :] for q in range(3))
            for i in range(chips - 2, -1, -1):
                near = whole[i, chunk, 2, at, :]
                sum_d = whole[i, chunk, 0, at, :] + near * sum_d
                sum_g = whole[i, chunk, 1, at, :] + near * sum_g
                keep = near * keep
            for q in range(3):
                out[q, to, :] = sum_d * color[q] + sum_g * shading
            out[3, to, :] = keep
    for chunk in ORDER:
        for j in range(chips):
            swap_of(chunk, j).wait_send()


def image(*operands):
    tall = pltpu.VMEM((DEEP, SPAN + 16, CY), F32)
    strip = pltpu.VMEM((DEEP, 16, CY), F32)
    return pl.pallas_call(
        image_kernel,
        out_shape=jax.ShapeDtypeStruct((4, CX, CY), F32),
        in_specs=[pl.BlockSpec(memory_space=pl.ANY)] * 10,
        out_specs=pl.BlockSpec(memory_space=pltpu.VMEM),
        scratch_shapes=[
            pltpu.VMEM((DEEP, PLANE, CY), F32),
            tall,
            tall,
            strip,
            strip,
            pltpu.VMEM((CZ + 2, CHUNK, CY), F32),
            pltpu.VMEM((CZ, CHUNK, CY), F32),
            pltpu.VMEM((CZ + 1, CHUNK, CY), F32),
            pltpu.VMEM((CHUNKS, TFS, 3, CHUNK, CY), F32),
            pltpu.VMEM((CHUNKS, 4, 3, CHUNK, CY), F32),
            pltpu.VMEM((4, CHUNKS, 3, CHUNK, CY), F32),
            pltpu.SMEM((3,), F32),
            *[pltpu.SMEM((TFS,), F32)] * 4,
            pltpu.SMEM((3, TFS), F32),
            pltpu.VMEM((8, CY), F32),
            pltpu.VMEM((2 * CY, 2 * CY), BF16),
            pltpu.VMEM((CY, 2 * CY), BF16),
            pltpu.SemaphoreType.DMA((9,)),
            pltpu.SemaphoreType.DMA,
            pltpu.SemaphoreType.DMA((3, 2)),
            pltpu.SemaphoreType.DMA((3, 2)),
            pltpu.SemaphoreType.DMA((CHUNKS, 2)),
            pltpu.SemaphoreType.DMA((CHUNKS, 2)),
            pltpu.SemaphoreType.DMA((CHUNKS, 4)),
            pltpu.SemaphoreType.DMA((CHUNKS, 4)),
            pltpu.SemaphoreType.DMA((CHUNKS, 3)),
            pltpu.SemaphoreType.DMA((CHUNKS, 3)),
        ],
        compiler_params=pltpu.CompilerParams(collective_id=0, has_side_effects=True, vmem_limit_bytes=32 << 20),
        name="image",
    )(*operands)


def shards(depth_cell, column_cell, row_cell, mass, counts, diffusion, tf_center, tf_sharp, tf_opacity, tf_shade, tf_color):
    forth, back, back_low, cosine = (jnp.asarray(table) for table in tables())
    cells = [cell.reshape(128, 128) for cell in (depth_cell, column_cell, row_cell)]
    extended = deposit(counts, *(pltpu.with_memory_space_constraint(x, pltpu.HBM) for x in (*cells, mass, forth)))
    return image(
        diffusion, tf_center, tf_sharp, tf_opacity, tf_shade, tf_color.T, cosine, back, back_low, extended
    )


def solution(mesh):
    brick = P("depth", "cols", None)
    placed = (brick,) * 4 + (P("depth", "cols"),) + (P(),) * 6
    return jax.shard_map(shards, mesh=mesh, in_specs=placed, out_specs=brick, check_vma=False)
```
